128 devices in a mesh: ctx: 16 (over y, x), exp: 8 (over z, core).
Axes of the slice: x: 4, y: 4, z: 4, core: 2. Of those that a mesh axis runs over, the one named last changes fastest.
Arguments:
- queries: bfloat16 [8192, 4096], P(('ctx', 'exp')), may hold values from -6 to 6
- rotated_key_heads: bfloat16 [8192, 512], P(('ctx', 'exp')), may hold values from -15 to 15
- stacked_value_heads: bfloat16 [8192, 512], P(('ctx', 'exp')), may hold values from -6 to 6
- moe_rows: bfloat16 [16384, 4096], P(('ctx', 'exp')), may hold values from -6 to 6
- expert_ids: int32 [16384, 8], P(('ctx', 'exp')), may hold values from 0 to 127, all different within a row; in each aligned block of 128 rows (0 to 127, 128 to 255, ...) at most 10 rows name the same one
- route_weights: float32 [16384, 8], P(('ctx', 'exp')), may hold values from 0.05 to 0.35
- w_gate: bfloat16 [128, 4096, 768], P(('ctx', 'exp')), may hold values from -0.09375 to 0.09375
- w_up: bfloat16 [128, 4096, 768], P(('ctx', 'exp')), may hold values from -0.09375 to 0.09375
- w_down: bfloat16 [128, 768, 4096], P(('ctx', 'exp')), may hold values from -0.21875 to 0.21875
Outputs:
- attended: bfloat16 [8192, 4096], P(('ctx', 'exp'))
- expert_mix: bfloat16 [16384, 4096], P(('ctx', 'exp'))
The draws below stay inside these ranges and needn't reach their ends.
Inputs may be any that keep to these rules, and one draw needn't show every extreme that they name: `expert_ids`: the 8 ids of a token are distinct. In each aligned block of 128 rows (the rows of one device) no expert is named by more than 10 rows, a bound that some block reaches.
All inputs are finite; a program needn't handle non-finite values.
Results may differ from the reference program's by a relative error of at most 0.0058.
Values may be sent and summed in bfloat16 or wider, within the bound.
A program may use at most 192 MiB of HBM per device.

```python
import math
import jax
import jax.numpy as jnp
import numpy as np
from jax import lax

D = 4096
QUERY_HEADS = 32
KEY_VALUE_HEADS = 4
HEAD_WIDTH = 128
FFE = 768
TOPK = 8
MOE_TOK = 128
SEQUENCE_LENGTH = 8192
MOE_TOKENS = 16384
EXPERTS = 128
MOST = 10
N_CTX = 16
N_EXP = 8


def draw_queries(key, part):
    random_noise_key = jax.random.fold_in(key, 11)
    base_offset = jax.random.normal(random_noise_key, (SEQUENCE_LENGTH, QUERY_HEADS * HEAD_WIDTH), jnp.float32)
    return jnp.clip(base_offset, -6.0, 6.0).astype(jnp.bfloat16)


def draw_rotated_key_heads(key, part):
    random_noise_key = jax.random.fold_in(key, 12)
    base_offset = 2.5 * jax.random.normal(random_noise_key, (SEQUENCE_LENGTH, KEY_VALUE_HEADS * HEAD_WIDTH), jnp.float32)
    return jnp.clip(base_offset, -15.0, 15.0).astype(jnp.bfloat16)


def block_levels(rng, dims, cuts, low, top_value):
    gain, own = 1.0, jax.random.fold_in(rng, 6)
    for dim, shards_of in cuts:
        heights = jnp.exp(jax.random.uniform(jax.random.fold_in(own, dim), (shards_of,), jnp.float32, low / len(cuts), top_value / len(cuts)))
        gain = gain * jnp.repeat(heights, dims[dim] // shards_of).reshape([-1 if axis == dim else 1 for axis in range(len(dims))])
    return gain


def routed_block(key, own, number, rows, count, top, most, lean):
    sequence = jax.random.permutation(key, count)
    packed, common = load_shares(count, rows * top, most, lean, True), load_shares(count, rows * top, most, lean, False)
    places = jnp.arange(count)

    def named(lengths, turn):
        used = int((lengths > 0).sum())
        fixed = max(1, used // 4)
        passed = fixed + (places - fixed + turn * (used - fixed)) % max(1, count - fixed)
        return jnp.zeros((count,), jnp.int32).at[sequence[jnp.where(places < fixed, places, passed)]].set(jnp.asarray(lengths, jnp.int32))

    lengths = jnp.where(number % 4 == 0, named(packed, number // 4), named(common, number - number // 4 - 1))
    mixed = jax.random.permutation(jax.random.fold_in(own, 3), count)
    donor, sink = mixed[0:count // 2 * 2:2], mixed[1:count // 2 * 2:2]
    slack = jnp.minimum(lengths[donor] - 1, most - lengths[sink]) // 2
    slack = jnp.where((donor == sequence[0]) | (sink == sequence[0]) | (lengths[sink] == 0), 0, jnp.maximum(slack, 0))
    passed = jax.random.randint(jax.random.fold_in(own, 4), (count // 2,), 0, 1 << 20) % (slack + 1)
    lengths = lengths.at[donor].add(-passed).at[sink].add(passed)
    members = jnp.searchsorted(jnp.cumsum(lengths), jnp.arange(rows * top), side="right").astype(jnp.int32)
    grid = members.reshape(top, rows).T
    grid = grid[jax.random.permutation(jax.random.fold_in(own, 1), rows)]
    turn = jax.random.randint(jax.random.fold_in(own, 2), (rows, 1), 0, top)
    return jnp.take_along_axis(grid, (jnp.arange(top)[None, :] + turn) % top, axis=1)


def load_shares(number_of, total, most, slope, full):
    portions = [(1 << 20) // math.isqrt(rank ** slope) + 1 for rank in range(1, number_of + 1)]
    largest = most if full else min(most, max(-(-total // number_of), total * portions[0] // sum(portions)))
    least = 1 if total - largest >= number_of - 1 else 0
    holding, surplus = [largest] + [least] * (number_of - 1), total - largest - least * (number_of - 1)
    while surplus > 0:
        free = [i for i in range(1, number_of) if holding[i] < largest] or [i for i in range(1, number_of) if holding[i] < most]
        pool, left = sum([portions[i] for i in free]), surplus
        for i in free:
            extra = min(most - holding[i], max(1, left * portions[i] // pool), surplus)
            holding[i] = holding[i] + extra
            surplus = surplus - extra
    return np.array(holding)


def normal_values(rng, extent, width, most, split=(), held_as=jnp.bfloat16):
    entries = jax.random.normal(rng, extent, jnp.float32) * width
    if len(split) > 0:
        entries = block_levels(rng, extent, split, -0.22, 0.18) * entries
    return jnp.clip(entries, min=-most, max=most).astype(held_as)


def setup_inputs(seed: int = 0) -> dict:
    keys = jax.random.split(jax.random.key(seed), 10)
    queries = draw_queries(jax.random.fold_in(keys[9], 71), 0)
    rotated_key_heads = draw_rotated_key_heads(jax.random.fold_in(keys[9], 71), 0)
    stacked_value_heads = normal_values(keys[2], (SEQUENCE_LENGTH, KEY_VALUE_HEADS * HEAD_WIDTH), 1.0, 6.0, ((0, 128),))
    moe_rows = normal_values(keys[3], (MOE_TOKENS, D), 1.0, 6.0, ((0, 128),))
    expert_ids_keys = jax.random.split(jax.random.fold_in(keys[4], 1), MOE_TOKENS // MOE_TOK)
    expert_ids_turns = jax.random.permutation(jax.random.fold_in(keys[4], 3), MOE_TOKENS // MOE_TOK)
    expert_ids = jax.vmap(lambda own, number: routed_block(jax.random.fold_in(keys[4], 2), own, number, MOE_TOK, EXPERTS, TOPK, MOST, 1))(expert_ids_keys, expert_ids_turns).reshape((MOE_TOKENS, TOPK))
    route_weights = jnp.clip(0.05 + 0.29999999 * jax.random.uniform(keys[5], (MOE_TOKENS, TOPK), jnp.float32) ** block_levels(keys[5], (MOE_TOKENS, TOPK), ((0, 128),), -0.2, 0.2), 0.05, 0.35)
    w_gate = normal_values(keys[6], (EXPERTS, D, FFE), D ** -0.5, 0.09375, ((0, 128),))
    w_up = normal_values(keys[7], (EXPERTS, D, FFE), D ** -0.5, 0.09375, ((0, 128),))
    w_down = normal_values(keys[8], (EXPERTS, FFE, D), FFE ** -0.5, 0.21875, ((0, 128),))
    return dict(queries=queries, rotated_key_heads=rotated_key_heads, stacked_value_heads=stacked_value_heads, moe_rows=moe_rows, expert_ids=expert_ids, route_weights=route_weights, w_gate=w_gate, w_up=w_up, w_down=w_down)


def attention(queries, rotated_key_heads, stacked_value_heads):
    span_length = queries.shape[0]
    query_grid = queries.reshape(span_length, QUERY_HEADS, HEAD_WIDTH)
    key_lattice = rotated_key_heads.reshape(span_length, KEY_VALUE_HEADS, HEAD_WIDTH)
    value_lattice = stacked_value_heads.reshape(span_length, KEY_VALUE_HEADS, HEAD_WIDTH)
    group_width = QUERY_HEADS // KEY_VALUE_HEADS
    positions = jnp.arange(span_length, dtype=jnp.int32)
    causal = positions[None, :] <= positions[:, None]
    scale_factor = 1.0 / (HEAD_WIDTH ** 0.5)

    def one_head(head):
        query_head = lax.dynamic_index_in_dim(query_grid, head, 1, keepdims=False)
        key_head = lax.dynamic_index_in_dim(key_lattice, head // group_width, 1, keepdims=False)
        value_head = lax.dynamic_index_in_dim(value_lattice, head // group_width, 1, keepdims=False)
        scores = jnp.dot(query_head, key_head.T, preferred_element_type=jnp.float32) * scale_factor
        scores = jnp.where(causal, scores, -1e30)
        row_max = jnp.max(scores, axis=1, keepdims=True)
        probs = jnp.where(causal, jnp.exp(scores - row_max), 0.0).astype(jnp.bfloat16)
        denominator = jnp.sum(probs.astype(jnp.float32), axis=1)
        summed = jnp.dot(probs, value_head, preferred_element_type=jnp.float32)
        return (summed / denominator[:, None]).astype(jnp.bfloat16)

    heads_out = lax.map(one_head, jnp.arange(QUERY_HEADS, dtype=jnp.int32))
    return jnp.transpose(heads_out, (1, 0, 2)).reshape(span_length, QUERY_HEADS * HEAD_WIDTH)


def reference(queries, rotated_key_heads, stacked_value_heads, moe_rows, expert_ids, route_weights, w_gate, w_up, w_down):
    attended = attention(queries, rotated_key_heads, stacked_value_heads)
    total_rows = moe_rows.shape[0]
    pair_count = total_rows * TOPK
    flat_ids = expert_ids.reshape(pair_count)
    padded_rows = jnp.concatenate([moe_rows, jnp.zeros((1, D), moe_rows.dtype)], 0)
    padded_weights = jnp.concatenate([route_weights.reshape(pair_count), jnp.zeros((1,), route_weights.dtype)], 0)
    limit = MOST * N_CTX * N_EXP

    def add_expert(index, summed):
        selected = jnp.nonzero(flat_ids == index, size=limit, fill_value=pair_count)[0].astype(jnp.int32)
        token_index = selected // TOPK
        inputs = padded_rows[token_index]
        gate_in = jnp.dot(inputs, w_gate[index], preferred_element_type=jnp.float32)
        up_in = jnp.dot(inputs, w_up[index], preferred_element_type=jnp.float32)
        hidden = (jax.nn.silu(gate_in) * up_in).astype(jnp.bfloat16)
        output = jnp.dot(hidden, w_down[index], preferred_element_type=jnp.float32).astype(jnp.bfloat16)
        scaled = padded_weights[selected][:, None] * output.astype(jnp.float32)
        return summed.at[token_index].add(scaled)

    summed = lax.fori_loop(0, EXPERTS, add_expert, jnp.zeros((total_rows + 1, D), jnp.float32))
    return (attended, summed[:total_rows].astype(jnp.bfloat16))
```

```python
import math

import jax
import jax.numpy as jnp
import numpy as np
from jax import lax
from jax.experimental import pallas as pl
from jax.experimental.pallas import tpu as pltpu
from jax.sharding import PartitionSpec as P

MESH = pl.DeviceIdType.MESH
BF = jnp.bfloat16
F32 = jnp.float32
D = 4096
FFE = 768
TOKENS = 128
SEQ = 64
PARTS = ((0, 0, 1536), (1, 1536, 1280), (2, 2816, 1280))
STEPS = (1, 3, 2)


def plane_offset(axis, i):
    d = [i // 4 % 4, i % 4]
    d.insert(axis, 0)
    return tuple(d) + (i // 16,)


def line_offset(axis, m):
    d = [0, 0, 0, 0]
    d[axis] = m
    return tuple(d)


def shuffled(core):
    order = [(p, i) for p in range(3) for i in range(16 * core, 16 * core + 16)]
    np.random.RandomState(3 + core).shuffle(order)
    return [(int(p), int(i)) for p, i in order if i > 0]


PEERS = sorted({plane_offset(p, i) for p in range(3) for i in range(1, 32)})


def place():
    c = lax.axis_index("ctx")
    e = lax.axis_index("exp")
    return c % 4, c // 4, e // 2, e % 2


def device(x, y, z, c):
    return (y * 4 + x, z * 2 + c)


def moved(d):
    x, y, z, c = place()
    return device((x + d[0]) % 4, (y + d[1]) % 4, (z + d[2]) % 4, (c + d[3]) % 2)


def moved_back(d):
    return moved(((-d[0]) % 4, (-d[1]) % 4, (-d[2]) % 4, d[3]))


def greet_all():
    barrier = pltpu.get_barrier_semaphore()
    for d in PEERS:
        pl.semaphore_signal(barrier, inc=1, device_id=moved(d), device_id_type=MESH)


def await_all():
    pl.semaphore_wait(pltpu.get_barrier_semaphore(), len(PEERS))


def remote(src, dst, send, recv, target):
    return pltpu.make_async_remote_copy(
        src_ref=src, dst_ref=dst, send_sem=send, recv_sem=recv, device_id=target, device_id_type=MESH
    )


def owners(axis):
    x, y, z, c = place()
    i = lax.broadcasted_iota(jnp.int32, (32, TOKENS), 0)
    d = [i // 4 % 4, i % 4]
    d.insert(axis, 0)
    chip = ((y + d[1]) % 4 * 4 + (x + d[0]) % 4) * 4 + (z + d[2]) % 4
    return (chip * 2 + (c + i // 16) % 2).astype(F32)


def ranks(ids, owner):
    named = jnp.zeros((32, TOKENS), F32)
    for k in range(8):
        named = named + jnp.where(ids[k : k + 1, :] == owner, 1.0, 0.0)
    shape = (TOKENS, TOKENS)
    before = lax.broadcasted_iota(jnp.int32, shape, 0) < lax.broadcasted_iota(jnp.int32, shape, 1)
    rank = jnp.dot(named.astype(BF), jnp.where(before, 1.0, 0.0).astype(BF), preferred_element_type=F32)
    return jnp.where(named > 0.5, rank, -1.0)


def spread(a):
    return jnp.broadcast_to(a[:, None, :], (32, 8, TOKENS)).reshape(256, TOKENS)


def line_index():
    return lax.broadcasted_iota(jnp.int32, (256, TOKENS), 0) % 8


def slot_masks(rank, m):
    row, line = spread(rank), line_index()
    early = row == line.astype(F32)
    late = (row == (8 + line % 2).astype(F32)) & (line // 2 == m)
    return early, late


def reorder(axis, forward):
    a = lax.broadcasted_iota(jnp.int32, (128, 128), 0 if forward else 1)
    b = lax.broadcasted_iota(jnp.int32, (128, 128), 1 if forward else 0)
    dx, dy, dz, s = a // 32, a // 8 % 4, a // 2 % 4, a % 2
    there = (dy * 4 + dz) * 8 + dx * 2 + s if axis == 0 else (dx * 4 + dz) * 8 + dy * 2 + s
    return jnp.where(there == b, 1.0, 0.0).astype(BF)


def kernel(
    q_ref, k_ref, v_ref, rows_ref, ids_ref, weight_ref, gate_ref, up_ref, down_ref,
    att_ref, mix_ref, recv_a, recv_b, recv_c, came_a, came_b, came_c,
    line_a, line_b, line_c, pack_a, pack_b, pack_c, ids_here, weights_here, info, meta, late_hot,
    kv, queries, v_turned, heads_out, work, gate, up, down, hidden, land, mixing, sum_a, sum_b, sum_c, own_sum,
    send_sem, recv_sem, line_send, line_recv, meta_send, meta_recv, in_send, in_recv,
    kv_send, kv_recv, core_send, core_recv, out_send, out_recv, local_sem,
    load_sem, w_sem, back_send, back_recv, sum_send, sum_recv, land_sem,
):
    x, y, z, c = place()
    ctx = y * 4 + x
    lines, packs, recvs = (line_a, line_b, line_c), (pack_a, pack_b, pack_c), (recv_a, recv_b, recv_c)
    cames, sums = (came_a, came_b, came_c), (sum_a, sum_b, sum_c)
    greet_all()
    small = [
        pltpu.make_async_copy(ids_ref, ids_here, land_sem.at[0]),
        pltpu.make_async_copy(weight_ref, weights_here, land_sem.at[1]),
    ]
    for copy in small:
        copy.start()
    mine = [
        pltpu.make_async_copy(rows_ref.at[:, at : at + width], lines[axis].at[pl.ds(0, TOKENS)], local_sem.at[7 + axis])
        for axis, at, width in PARTS
    ]
    for copy in mine:
        copy.start()
    for copy in small:
        copy.wait()
    info[0:8, :] = ids_here[...].astype(F32)
    info[8:16, :] = weights_here[...]
    await_all()

    along = {}
    for n, m in enumerate(STEPS):
        for axis, at, width in PARTS:
            target = moved(line_offset(axis, m))
            i = 3 * n + axis
            told = remote(info, meta.at[axis, m], meta_send.at[i], meta_recv.at[i], target)
            told.start()
            data = remote(
                rows_ref.at[:, at : at + width], lines[axis].at[pl.ds(TOKENS * m, TOKENS)],
                line_send.at[i], line_recv.at[i], target,
            )
            data.start()
            along[axis, m] = (told, data)

    first = []
    for dz in range(1, 4):
        zt = (z + dz) % 4
        target = device(x, y, zt, c)
        for n, (src, dst) in enumerate(
            (
                (k_ref.at[:, pl.ds(zt * 128, 128)], kv.at[ctx, z, c, :, pl.ds(0, 128)]),
                (v_ref.at[:, pl.ds(zt * 128, 128)], kv.at[ctx, z, c, :, pl.ds(128, 128)]),
                (q_ref.at[:, pl.ds(zt * 1024, 1024)], queries.at[z]),
            )
        ):
            i = (dz - 1) * 3 + n
            first.append(remote(src, dst, in_send.at[i], in_recv.at[i], target))
            first[-1].start()
    own = (
        (k_ref.at[:, pl.ds(z * 128, 128)], kv.at[ctx, z, c, :, pl.ds(0, 128)]),
        (v_ref.at[:, pl.ds(z * 128, 128)], kv.at[ctx, z, c, :, pl.ds(128, 128)]),
        (q_ref.at[:, pl.ds(z * 1024, 1024)], queries.at[z]),
    )
    for i, (src, dst) in enumerate(own):
        first.append(pltpu.make_async_copy(src, dst, local_sem.at[i]))
        first[-1].start()

    weights = [
        pltpu.make_async_copy(gate_ref.at[0], gate, w_sem.at[0]),
        pltpu.make_async_copy(up_ref.at[0], up, w_sem.at[1]),
        pltpu.make_async_copy(down_ref.at[0], down, w_sem.at[2]),
    ]
    for copy in weights:
        copy.start()

    for m in (0,) + STEPS:
        for axis, at, width in PARTS:
            if m == 0:
                meta[axis, 0] = info[...]
                mine[axis].wait()
            else:
                for copy in along[axis, m]:
                    copy.wait()
            early, late = slot_masks(ranks(meta[axis, m], owners(axis)), m)
            hot = jnp.where(early, 1.0, 0.0).astype(BF)
            late_hot[axis, :, TOKENS * m : TOKENS * (m + 1)] = jnp.where(late, 1.0, 0.0).astype(BF)
            packs[axis][m] = jnp.dot(
                hot, lines[axis][TOKENS * m : TOKENS * (m + 1), :], preferred_element_type=F32
            ).astype(BF)
    for copy in first:
        copy.wait()
    for k in range(1, 16):

        @pl.when(ctx + k < 16)
        def _():
            there = ctx + k
            remote(
                kv.at[ctx, :, c], kv.at[ctx, :, c], kv_send.at[k - 1], kv_recv.at[k - 1], (there, z * 2 + c)
            ).start()

    for axis, at, width in PARTS:
        packs[axis][4] = jnp.dot(late_hot[axis], lines[axis][...], preferred_element_type=F32).astype(BF)

    sends = ([], [])
    stays = []
    for core in range(2):
        for axis, i in shuffled(core):
            cut = pl.ds(8 * i, 8)
            n = 31 * axis + i - 1
            sends[core].append(
                remote(
                    packs[axis].at[:, cut], recvs[axis].at[:, cut],
                    send_sem.at[n], recv_sem.at[n], moved(plane_offset(axis, i)),
                )
            )
            sends[core][-1].start()
    for axis in range(3):
        cut = pl.ds(0, 8)
        stays.append(pltpu.make_async_copy(packs[axis].at[:, cut], recvs[axis].at[:, cut], local_sem.at[3 + axis]))
        stays[-1].start()

    for k in range(1, 16):
        copy = remote(
            kv.at[ctx, :, c], kv.at[ctx, :, c], kv_send.at[k - 1], kv_recv.at[k - 1], (ctx, z * 2 + c)
        )

        @pl.when(ctx >= k)
        def _():
            copy.wait_recv()

        @pl.when(ctx + k < 16)
        def _():
            copy.wait_send()

    def core_copy(j):
        return remote(
            kv.at[j, :, c], kv.at[j, :, c], core_send.at[j], core_recv.at[j], device(x, y, z, 1 - c)
        )

    def core_start(j, carry):
        core_copy(j).start()
        return carry

    def core_wait(j, carry):
        core_copy(j).wait()
        return carry

    lax.fori_loop(0, ctx + 1, core_start, 0)
    lax.fori_loop(0, ctx + 1, core_wait, 0)

    def turn(j, carry):
        block = kv[j].reshape(512, 256)
        v_turned[j] = block[:, 128:256].astype(F32).T.astype(BF)
        return carry

    lax.fori_loop(0, ctx + 1, turn, 0)
    factor = math.log2(math.e) / math.sqrt(128.0)
    column = lax.broadcasted_iota(jnp.int32, (512, 256), 1)
    allowed = lax.broadcasted_iota(jnp.int32, (512, 256), 0) <= (column // 64 * 2 + c) * 64 + column % 64

    def head(h, carry):
        cut = pl.ds(pl.multiple_of(h * 128, 128), 128)
        q = queries[:, :, cut].reshape(256, 128)

        def step(j, state, masked):
            row_max, row_sum, total = state
            key = kv[j].reshape(512, 256)[:, 0:128]
            score = lax.dot_general(key, q, (((1,), (1,)), ((), ())), preferred_element_type=F32) * factor
            if masked:
                score = jnp.where(allowed, score, -1e30)
            new_max = jnp.maximum(row_max, jnp.max(score, axis=0, keepdims=True))
            prob = jnp.exp2(score - new_max)
            old = jnp.exp2(row_max - new_max)
            row_sum = row_sum * old + jnp.sum(prob, axis=0, keepdims=True)
            total = total * old + jnp.dot(v_turned[j], prob.astype(BF), preferred_element_type=F32)
            return (new_max, row_sum, total)

        state = (
            jnp.full((1, 256), -1e30, F32),
            jnp.zeros((1, 256), F32),
            jnp.zeros((128, 256), F32),
        )
        state = step(ctx, state, True)
        state = lax.fori_loop(0, ctx, lambda j, s: step(j, s, False), state)
        result = (state[2] / state[1]).T
        heads_out[:, :, cut] = result.reshape(4, 64, 128).astype(BF)
        return carry

    lax.fori_loop(0, 8, head, 0)
    last = []
    for dz in range(1, 4):
        zt = (z + dz) % 4
        last.append(
            remote(
                heads_out.at[zt], att_ref.at[:, pl.ds(z * 1024, 1024)],
                out_send.at[dz - 1], out_recv.at[dz - 1], device(x, y, zt, c),
            )
        )
        last[-1].start()
    last.append(pltpu.make_async_copy(heads_out.at[z], att_ref.at[:, pl.ds(z * 1024, 1024)], local_sem.at[6]))
    last[-1].start()

    def load(core):
        at = 128 * core
        for dx in range(4):
            pltpu.make_async_copy(
                recv_a.at[dx, pl.ds(at, 128)], work.at[pl.ds(128 * dx, 128), 0:1536], load_sem.at[0]
            ).start()
        pltpu.make_async_copy(recv_a.at[4, pl.ds(at, 128)], work.at[pl.ds(512, 128), 0:1536], load_sem.at[0]).start()
        for n in range(16):
            pltpu.make_async_copy(
                recv_b.at[n % 4, pl.ds(at + n // 4 * 32, 32)], work.at[pl.ds(32 * n, 32), 1536:2816], load_sem.at[0]
            ).start()
        pltpu.make_async_copy(recv_b.at[4, pl.ds(at, 128)], work.at[pl.ds(512, 128), 1536:2816], load_sem.at[0]).start()

        def piece(n, carry):
            pltpu.make_async_copy(
                recv_c.at[n % 4, pl.ds(pl.multiple_of(at + n // 4 * 8, 8), 8)],
                work.at[pl.ds(pl.multiple_of(8 * n, 8), 8), 2816:4096],
                load_sem.at[0],
            ).start()
            return carry

        lax.fori_loop(0, 64, piece, 0)
        pltpu.make_async_copy(recv_c.at[4, pl.ds(at, 128)], work.at[pl.ds(512, 128), 2816:4096], load_sem.at[0]).start()

    returns = []
    for core in range(2):
        for copy in sends[core]:
            copy.wait_recv()
        if core == 0:
            for copy in stays:
                copy.wait()
        load(core)
        pltpu.make_async_copy(work, work, load_sem.at[0]).wait()
        if core == 0:
            weights[0].wait()
            weights[1].wait()
        for axis, at, width in PARTS[:2]:
            work[512:640, at : at + width] = jnp.dot(
                reorder(axis, True), work[512:640, at : at + width], preferred_element_type=F32
            ).astype(BF)

        def inner(n, carry):
            cut = pl.ds(pl.multiple_of(n * 256, 256), 256)
            a = jnp.dot(work[...], gate[:, cut], preferred_element_type=F32)
            b = jnp.dot(work[...], up[:, cut], preferred_element_type=F32)
            hidden[:, cut] = (a / (1.0 + jnp.exp(-a)) * b).astype(BF)
            return carry

        lax.fori_loop(0, 3, inner, 0)
        if core == 0:
            weights[2].wait()
        for copy in sends[core]:
            copy.wait_send()
        for axis, at, width in PARTS:
            ref = packs[axis]

            def outer(n, carry):
                cut = pl.ds(pl.multiple_of(n * 256, 256), 256)
                from_cut = pl.ds(pl.multiple_of(at + n * 256, 256), 256)
                value = jnp.dot(hidden[...], down[:, from_cut], preferred_element_type=F32)
                row = 128 * core
                if axis == 0:
                    for dx in range(4):
                        ref[dx, row : row + 128, cut] = value[128 * dx : 128 * (dx + 1)].astype(BF)
                elif axis == 1:
                    for n2 in range(16):
                        to = row + n2 // 4 * 32
                        ref[n2 % 4, to : to + 32, cut] = value[32 * n2 : 32 * (n2 + 1)].astype(BF)
                else:
                    for n2 in range(64):
                        to = row + n2 // 4 * 8
                        ref[n2 % 4, to : to + 8, cut] = value[8 * n2 : 8 * (n2 + 1)].astype(BF)
                late = value[512:640].astype(BF)
                if axis < 2:
                    late = jnp.dot(reorder(axis, False), late, preferred_element_type=F32).astype(BF)
                ref[4, row : row + 128, cut] = late
                return carry

            lax.fori_loop(0, width // 256, outer, 0)
        for axis, i in shuffled(core):
            cut = pl.ds(8 * i, 8)
            n = 31 * axis + i - 1
            returns.append(
                remote(
                    packs[axis].at[:, cut], cames[axis].at[:, cut],
                    back_send.at[n], back_recv.at[n], moved_back(plane_offset(axis, i)),
                )
            )
            returns[-1].start()
        if core == 0:
            for axis in range(3):
                cut = pl.ds(0, 8)
                returns.append(
                    pltpu.make_async_copy(packs[axis].at[:, cut], cames[axis].at[:, cut], local_sem.at[3 + axis])
                )
                returns[-1].start()

    for axis, at, width in PARTS:
        for m in range(4):
            early, late = slot_masks(ranks(meta[axis, m], owners(axis)), m)
            value = jnp.zeros((32, TOKENS), F32)
            for k in range(8):
                value = value + jnp.where(
                    meta[axis, m, k : k + 1, :] == owners(axis), meta[axis, m, 8 + k : 9 + k, :], 0.0
                )
            value = spread(value)
            for n, mask in enumerate((early, late)):
                turned = jnp.where(mask, value, 0.0).T
                high = turned.astype(BF)
                mixing[axis, m, 0:TOKENS, 256 * n : 256 * (n + 1)] = high
                mixing[axis, m, TOKENS : 2 * TOKENS, 256 * n : 256 * (n + 1)] = (turned - high.astype(F32)).astype(BF)
    for copy in returns:
        copy.wait()

    tiles = [(axis, n) for axis, at, width in PARTS for n in range(width // 256)]

    def fetch(t):
        axis, n = tiles[t]
        return pltpu.make_async_copy(
            cames[axis].at[:, :, 256 * n : 256 * (n + 1)], land.at[t % 2], land_sem.at[t % 2]
        )

    parts = []
    fetch(0).start()
    for t, (axis, n) in enumerate(tiles):
        if t + 1 < len(tiles):
            fetch(t + 1).start()
        fetch(t).wait()
        cut = slice(256 * n, 256 * (n + 1))
        for m in STEPS + (0,):
            both = jnp.dot(mixing[axis, m, :, 0:256], land[t % 2, m], preferred_element_type=F32)
            both = both + jnp.dot(mixing[axis, m, :, 256:512], land[t % 2, 4], preferred_element_type=F32)
            total = both[0:TOKENS] + both[TOKENS : 2 * TOKENS]
            if m == 0:
                at = PARTS[axis][1] + 256 * n
                own_sum[:, at : at + 256] = total
            else:
                lines[axis][TOKENS * m : TOKENS * (m + 1), cut] = total.astype(BF)
        if n == PARTS[axis][2] // 256 - 1:
            for s, m in enumerate(STEPS):
                i = 3 * s + axis
                parts.append(
                    remote(
                        lines[axis].at[pl.ds(TOKENS * m, TOKENS)], sums[axis].at[s], sum_send.at[i], sum_recv.at[i],
                        moved_back(line_offset(axis, m)),
                    )
                )
                parts[-1].start()
    for copy in last:
        copy.wait()
    for copy in parts:
        copy.wait()
    for axis, at, width in PARTS:
        total = own_sum[:, at : at + width]
        for s in range(3):
            total = total + sums[axis][s].astype(F32)
        work[0:TOKENS, at : at + width] = total.astype(BF)
    result = pltpu.make_async_copy(work.at[pl.ds(0, TOKENS)], mix_ref, local_sem.at[0])
    result.start()
    result.wait()


def body(
    queries, rotated_key_heads, stacked_value_heads, moe_rows, expert_ids, route_weights, w_gate, w_up, w_down
):
    hbm = pl.BlockSpec(memory_space=pl.ANY)
    dma = pltpu.SemaphoreType.DMA
    widths = [width for _, _, width in PARTS]
    results = pl.pallas_call(
        kernel,
        out_shape=(jax.ShapeDtypeStruct((SEQ, D), BF), jax.ShapeDtypeStruct((TOKENS, D), BF))
        + tuple(jax.ShapeDtypeStruct((5, 256, w), BF) for w in widths) * 2,
        in_specs=[hbm] * 9,
        out_specs=(hbm,) * 8,
        scratch_shapes=[pltpu.VMEM((4 * TOKENS, w), BF) for w in widths]
        + [pltpu.VMEM((5, 256, w), BF) for w in widths]
        + [
            pltpu.VMEM((8, TOKENS), jnp.int32),
            pltpu.VMEM((8, TOKENS), F32),
            pltpu.VMEM((16, TOKENS), F32),
            pltpu.VMEM((3, 4, 16, TOKENS), F32),
            pltpu.VMEM((3, 256, 4 * TOKENS), BF),
            pltpu.VMEM((16, 4, 2, SEQ, 256), BF),
            pltpu.VMEM((4, SEQ, 1024), BF),
            pltpu.VMEM((16, 128, 512), BF),
            pltpu.VMEM((4, SEQ, 1024), BF),
            pltpu.VMEM((640, D), BF),
            pltpu.VMEM((D, FFE), BF),
            pltpu.VMEM((D, FFE), BF),
            pltpu.VMEM((FFE, D), BF),
            pltpu.VMEM((640, FFE), BF),
            pltpu.VMEM((2, 5, 256, 256), BF),
            pltpu.VMEM((3, 4, 2 * TOKENS, 512), BF),
        ]
        + [pltpu.VMEM((3, TOKENS, w), BF) for w in widths]
        + [pltpu.VMEM((TOKENS, D), F32)]
        + [dma((n,)) for n in (93, 93, 9, 9, 9, 9, 9, 9, 15, 15, 16, 16, 3, 3, 10)]
        + [dma((n,)) for n in (1, 3, 93, 93, 9, 9, 2)],
        compiler_params=pltpu.CompilerParams(
            collective_id=0, has_side_effects=True, vmem_limit_bytes=62 * 2**20
        ),
        name="attend_and_mix",
    )(
        queries, rotated_key_heads, stacked_value_heads, moe_rows, expert_ids.T, route_weights.T,
        w_gate, w_up, w_down,
    )
    return results[0], results[1]


def solution(mesh):
    rows = P(("ctx", "exp"), None)
    cube = P(("ctx", "exp"), None, None)
    return jax.shard_map(
        body,
        mesh=mesh,
        in_specs=(rows,) * 6 + (cube,) * 3,
        out_specs=(rows, rows),
        check_vma=False,
    )
```

```python
import math

import jax
import jax.numpy as jnp
import numpy as np
from jax import lax
from jax.experimental import pallas as pl
from jax.experimental.pallas import tpu as pltpu
from jax.sharding import PartitionSpec as P

MESH = pl.DeviceIdType.MESH
BF = jnp.bfloat16
F32 = jnp.float32
D = 4096
FFE = 768
TOKENS = 128
SEQ = 64
PARTS = ((0, 0, 1536), (1, 1536, 1280), (2, 2816, 1280))
STEPS = (1, 3, 2)


def plane_offset(axis, i):
    d = [i // 4 % 4, i % 4]
    d.insert(axis, 0)
    return tuple(d) + (i // 16,)


def line_offset(axis, m):
    d = [0, 0, 0, 0]
    d[axis] = m
    return tuple(d)


def shuffled(core):
    order = [(p, i) for p in range(3) for i in range(16 * core, 16 * core + 16)]
    np.random.RandomState(3 + core).shuffle(order)
    return [(int(p), int(i)) for p, i in order if i > 0]


PEERS = sorted({plane_offset(p, i) for p in range(3) for i in range(1, 32)})


def place():
    c = lax.axis_index("ctx")
    e = lax.axis_index("exp")
    return c % 4, c // 4, e // 2, e % 2


def device(x, y, z, c):
    return (y * 4 + x, z * 2 + c)


def moved(d):
    x, y, z, c = place()
    return device((x + d[0]) % 4, (y + d[1]) % 4, (z + d[2]) % 4, (c + d[3]) % 2)


def moved_back(d):
    return moved(((-d[0]) % 4, (-d[1]) % 4, (-d[2]) % 4, d[3]))


def greet_all():
    barrier = pltpu.get_barrier_semaphore()
    for d in PEERS:
        pl.semaphore_signal(barrier, inc=1, device_id=moved(d), device_id_type=MESH)


def await_all():
    pl.semaphore_wait(pltpu.get_barrier_semaphore(), len(PEERS))


def remote(src, dst, send, recv, target):
    return pltpu.make_async_remote_copy(
        src_ref=src, dst_ref=dst, send_sem=send, recv_sem=recv, device_id=target, device_id_type=MESH
    )


def owners(axis):
    x, y, z, c = place()
    i = lax.broadcasted_iota(jnp.int32, (32, TOKENS), 0)
    d = [i // 4 % 4, i % 4]
    d.insert(axis, 0)
    chip = ((y + d[1]) % 4 * 4 + (x + d[0]) % 4) * 4 + (z + d[2]) % 4
    return (chip * 2 + (c + i // 16) % 2).astype(F32)


def ranks(ids, owner):
    named = jnp.zeros((32, TOKENS), F32)
    for k in range(8):
        named = named + jnp.where(ids[k : k + 1, :] == owner, 1.0, 0.0)
    shape = (TOKENS, TOKENS)
    before = lax.broadcasted_iota(jnp.int32, shape, 0) < lax.broadcasted_iota(jnp.int32, shape, 1)
    rank = jnp.dot(named.astype(BF), jnp.where(before, 1.0, 0.0).astype(BF), preferred_element_type=F32)
    return jnp.where(named > 0.5, rank, -1.0)


def spread(a):
    return jnp.broadcast_to(a[:, None, :], (32, 8, TOKENS)).reshape(256, TOKENS)


def line_index():
    return lax.broadcasted_iota(jnp.int32, (256, TOKENS), 0) % 8


def slot_masks(rank, m):
    row, line = spread(rank), line_index()
    early = row == line.astype(F32)
    late = (row == (8 + line % 2).astype(F32)) & (line // 2 == m)
    return early, late


def reorder(axis, forward):
    a = lax.broadcasted_iota(jnp.int32, (128, 128), 0 if forward else 1)
    b = lax.broadcasted_iota(jnp.int32, (128, 128), 1 if forward else 0)
    dx, dy, dz, s = a // 32, a // 8 % 4, a // 2 % 4, a % 2
    there = (dy * 4 + dz) * 8 + dx * 2 + s if axis == 0 else (dx * 4 + dz) * 8 + dy * 2 + s
    return jnp.where(there == b, 1.0, 0.0).astype(BF)


def kernel(
    q_ref, k_ref, v_ref, rows_ref, ids_ref, weight_ref, gate_ref, up_ref, down_ref,
    att_ref, mix_ref, recv_a, recv_b, recv_c, came_a, came_b, came_c,
    line_a, line_b, line_c, pack_a, pack_b, pack_c, ids_here, weights_here, info, meta, late_hot,
    kv, queries, v_turned, heads_out, work, gate, up, down, hidden, land, mixing, sum_a, sum_b, sum_c, own_sum,
    send_sem, recv_sem, line_send, line_recv, meta_send, meta_recv, in_send, in_recv,
    kv_send, kv_recv, core_send, core_recv, out_send, out_recv, local_sem,
    load_sem, w_sem, back_send, back_recv, sum_send, sum_recv, land_sem,
):
    x, y, z, c = place()
    ctx = y * 4 + x
    lines, packs, recvs = (line_a, line_b, line_c), (pack_a, pack_b, pack_c), (recv_a, recv_b, recv_c)
    cames, sums = (came_a, came_b, came_c), (sum_a, sum_b, sum_c)
    greet_all()
    small = [
        pltpu.make_async_copy(ids_ref, ids_here, land_sem.at[0]),
        pltpu.make_async_copy(weight_ref, weights_here, land_sem.at[1]),
    ]
    for copy in small:
        copy.start()
    mine = [
        pltpu.make_async_copy(rows_ref.at[:, at : at + width], lines[axis].at[pl.ds(0, TOKENS)], local_sem.at[7 + axis])
        for axis, at, width in PARTS
    ]
    for copy in mine:
        copy.start()
    for copy in small:
        copy.wait()
    info[0:8, :] = ids_here[...].astype(F32)
    info[8:16, :] = weights_here[...]
    await_all()

    first = []
    for dz in range(4):
        zt = (z + dz) % 4
        for n, ref in enumerate((k_ref, v_ref)):
            there = ref.at[:, pl.ds(zt * 128, 128)]
            here = kv.at[ctx, z, c, :, pl.ds(128 * n, 128)]
            if dz == 0:
                first.append(pltpu.make_async_copy(there, here, local_sem.at[n]))
            else:
                i = (dz - 1) * 3 + n
                first.append(remote(there, here, in_send.at[i], in_recv.at[i], device(x, y, zt, c)))
            first[-1].start()

    along = {}
    for n, m in enumerate(STEPS):
        for axis, at, width in PARTS:
            target = moved(line_offset(axis, m))
            i = 3 * n + axis
            told = remote(info, meta.at[axis, m], meta_send.at[i], meta_recv.at[i], target)
            told.start()
            data = remote(
                rows_ref.at[:, at : at + width], lines[axis].at[pl.ds(TOKENS * m, TOKENS)],
                line_send.at[i], line_recv.at[i], target,
            )
            data.start()
            along[axis, m] = (told, data)

    for copy in first:
        copy.wait()
    for k in range(1, 16):

        @pl.when(ctx + k < 16)
        def _():
            there = ctx + k
            remote(
                kv.at[ctx, :, c], kv.at[ctx, :, c], kv_send.at[k - 1], kv_recv.at[k - 1], (there, z * 2 + c)
            ).start()

    weights = [
        pltpu.make_async_copy(gate_ref.at[0], gate, w_sem.at[0]),
        pltpu.make_async_copy(up_ref.at[0], up, w_sem.at[1]),
        pltpu.make_async_copy(down_ref.at[0], down, w_sem.at[2]),
    ]
    for copy in weights:
        copy.start()

    for m in (0,) + STEPS:
        for axis, at, width in PARTS:
            if m == 0:
                meta[axis, 0] = info[...]
                mine[axis].wait()
            else:
                for copy in along[axis, m]:
                    copy.wait()
            early, late = slot_masks(ranks(meta[axis, m], owners(axis)), m)
            hot = jnp.where(early, 1.0, 0.0).astype(BF)
            late_hot[axis, :, TOKENS * m : TOKENS * (m + 1)] = jnp.where(late, 1.0, 0.0).astype(BF)
            packs[axis][m] = jnp.dot(
                hot, lines[axis][TOKENS * m : TOKENS * (m + 1), :], preferred_element_type=F32
            ).astype(BF)
    for axis, at, width in PARTS:
        packs[axis][4] = jnp.dot(late_hot[axis], lines[axis][...], preferred_element_type=F32).astype(BF)

    sends = ([], [])
    stays = []
    for core in range(2):
        for axis, i in shuffled(core):
            cut = pl.ds(8 * i, 8)
            n = 31 * axis + i - 1
            sends[core].append(
                remote(
                    packs[axis].at[:, cut], recvs[axis].at[:, cut],
                    send_sem.at[n], recv_sem.at[n], moved(plane_offset(axis, i)),
                )
            )
            sends[core][-1].start()
    for axis in range(3):
        cut = pl.ds(0, 8)
        stays.append(pltpu.make_async_copy(packs[axis].at[:, cut], recvs[axis].at[:, cut], local_sem.at[3 + axis]))
        stays[-1].start()

    asked = []
    for dz in range(4):
        zt = (z + dz) % 4
        there = q_ref.at[:, pl.ds(zt * 1024, 1024)]
        if dz == 0:
            asked.append(pltpu.make_async_copy(there, queries.at[z], local_sem.at[2]))
        else:
            i = (dz - 1) * 3 + 2
            asked.append(remote(there, queries.at[z], in_send.at[i], in_recv.at[i], device(x, y, zt, c)))
        asked[-1].start()

    def load(core):
        at = 128 * core
        for dx in range(4):
            pltpu.make_async_copy(
                recv_a.at[dx, pl.ds(at, 128)], work.at[pl.ds(128 * dx, 128), 0:1536], load_sem.at[0]
            ).start()
        pltpu.make_async_copy(recv_a.at[4, pl.ds(at, 128)], work.at[pl.ds(512, 128), 0:1536], load_sem.at[0]).start()
        for n in range(16):
            pltpu.make_async_copy(
                recv_b.at[n % 4, pl.ds(at + n // 4 * 32, 32)], work.at[pl.ds(32 * n, 32), 1536:2816], load_sem.at[0]
            ).start()
        pltpu.make_async_copy(recv_b.at[4, pl.ds(at, 128)], work.at[pl.ds(512, 128), 1536:2816], load_sem.at[0]).start()

        def piece(n, carry):
            pltpu.make_async_copy(
                recv_c.at[n % 4, pl.ds(pl.multiple_of(at + n // 4 * 8, 8), 8)],
                work.at[pl.ds(pl.multiple_of(8 * n, 8), 8), 2816:4096],
                load_sem.at[0],
            ).start()
            return carry

        lax.fori_loop(0, 64, piece, 0)
        pltpu.make_async_copy(recv_c.at[4, pl.ds(at, 128)], work.at[pl.ds(512, 128), 2816:4096], load_sem.at[0]).start()

    returns = []
    for core in range(2):
        for copy in sends[core]:
            copy.wait_recv()
        if core == 0:
            for copy in stays:
                copy.wait()
        load(core)
        pltpu.make_async_copy(work, work, load_sem.at[0]).wait()
        if core == 0:
            weights[0].wait()
            weights[1].wait()
        for axis, at, width in PARTS[:2]:
            work[512:640, at : at + width] = jnp.dot(
                reorder(axis, True), work[512:640, at : at + width], preferred_element_type=F32
            ).astype(BF)

        def inner(n, carry):
            cut = pl.ds(pl.multiple_of(n * 256, 256), 256)
            a = jnp.dot(work[...], gate[:, cut], preferred_element_type=F32)
            b = jnp.dot(work[...], up[:, cut], preferred_element_type=F32)
            hidden[:, cut] = (a / (1.0 + jnp.exp(-a)) * b).astype(BF)
            return carry

        lax.fori_loop(0, 3, inner, 0)
        if core == 0:
            weights[2].wait()
        for copy in sends[core]:
            copy.wait_send()
        for axis, at, width in PARTS:
            ref = packs[axis]

            def outer(n, carry):
                cut = pl.ds(pl.multiple_of(n * 256, 256), 256)
                from_cut = pl.ds(pl.multiple_of(at + n * 256, 256), 256)
                value = jnp.dot(hidden[...], down[:, from_cut], preferred_element_type=F32)
                row = 128 * core
                if axis == 0:
                    for dx in range(4):
                        ref[dx, row : row + 128, cut] = value[128 * dx : 128 * (dx + 1)].astype(BF)
                elif axis == 1:
                    for n2 in range(16):
                        to = row + n2 // 4 * 32
                        ref[n2 % 4, to : to + 32, cut] = value[32 * n2 : 32 * (n2 + 1)].astype(BF)
                else:
                    for n2 in range(64):
                        to = row + n2 // 4 * 8
                        ref[n2 % 4, to : to + 8, cut] = value[8 * n2 : 8 * (n2 + 1)].astype(BF)
                late = value[512:640].astype(BF)
                if axis < 2:
                    late = jnp.dot(reorder(axis, False), late, preferred_element_type=F32).astype(BF)
                ref[4, row : row + 128, cut] = late
                return carry

            lax.fori_loop(0, width // 256, outer, 0)
        for axis, i in shuffled(core):
            cut = pl.ds(8 * i, 8)
            n = 31 * axis + i - 1
            returns.append(
                remote(
                    packs[axis].at[:, cut], cames[axis].at[:, cut],
                    back_send.at[n], back_recv.at[n], moved_back(plane_offset(axis, i)),
                )
            )
            returns[-1].start()
        if core == 0:
            for axis in range(3):
                cut = pl.ds(0, 8)
                returns.append(
                    pltpu.make_async_copy(packs[axis].at[:, cut], cames[axis].at[:, cut], local_sem.at[3 + axis])
                )
                returns[-1].start()

    for axis, at, width in PARTS:
        for m in range(4):
            early, late = slot_masks(ranks(meta[axis, m], owners(axis)), m)
            value = jnp.zeros((32, TOKENS), F32)
            for k in range(8):
                value = value + jnp.where(
                    meta[axis, m, k : k + 1, :] == owners(axis), meta[axis, m, 8 + k : 9 + k, :], 0.0
                )
            value = spread(value)
            for n, mask in enumerate((early, late)):
                turned = jnp.where(mask, value, 0.0).T
                high = turned.astype(BF)
                mixing[axis, m, 0:TOKENS, 256 * n : 256 * (n + 1)] = high
                mixing[axis, m, TOKENS : 2 * TOKENS, 256 * n : 256 * (n + 1)] = (turned - high.astype(F32)).astype(BF)
    for copy in asked:
        copy.wait()
    for k in range(1, 16):
        copy = remote(
            kv.at[ctx, :, c], kv.at[ctx, :, c], kv_send.at[k - 1], kv_recv.at[k - 1], (ctx, z * 2 + c)
        )

        @pl.when(ctx >= k)
        def _():
            copy.wait_recv()

        @pl.when(ctx + k < 16)
        def _():
            copy.wait_send()

    def core_copy(j):
        return remote(
            kv.at[j, :, c], kv.at[j, :, c], core_send.at[j], core_recv.at[j], device(x, y, z, 1 - c)
        )

    def core_start(j, carry):
        core_copy(j).start()
        return carry

    def core_wait(j, carry):
        core_copy(j).wait()
        return carry

    lax.fori_loop(0, ctx + 1, core_start, 0)
    lax.fori_loop(0, ctx + 1, core_wait, 0)

    def turn(j, carry):
        block = kv[j].reshape(512, 256)
        v_turned[j] = block[:, 128:256].astype(F32).T.astype(BF)
        return carry

    lax.fori_loop(0, ctx + 1, turn, 0)
    factor = math.log2(math.e) / math.sqrt(128.0)
    column = lax.broadcasted_iota(jnp.int32, (512, 256), 1)
    allowed = lax.broadcasted_iota(jnp.int32, (512, 256), 0) <= (column // 64 * 2 + c) * 64 + column % 64

    def head(h, carry):
        cut = pl.ds(pl.multiple_of(h * 128, 128), 128)
        q = queries[:, :, cut].reshape(256, 128)

        def step(j, state, masked):
            row_max, row_sum, total = state
            key = kv[j].reshape(512, 256)[:, 0:128]
            score = lax.dot_general(key, q, (((1,), (1,)), ((), ())), preferred_element_type=F32) * factor
            if masked:
                score = jnp.where(allowed, score, -1e30)
            new_max = jnp.maximum(row_max, jnp.max(score, axis=0, keepdims=True))
            prob = jnp.exp2(score - new_max)
            old = jnp.exp2(row_max - new_max)
            row_sum = row_sum * old + jnp.sum(prob, axis=0, keepdims=True)
            total = total * old + jnp.dot(v_turned[j], prob.astype(BF), preferred_element_type=F32)
            return (new_max, row_sum, total)

        state = (
            jnp.full((1, 256), -1e30, F32),
            jnp.zeros((1, 256), F32),
            jnp.zeros((128, 256), F32),
        )
        state = step(ctx, state, True)
        state = lax.fori_loop(0, ctx, lambda j, s: step(j, s, False), state)
        result = (state[2] / state[1]).T
        heads_out[:, :, cut] = result.reshape(4, 64, 128).astype(BF)
        return carry

    lax.fori_loop(0, 8, head, 0)
    last = []
    for dz in range(1, 4):
        zt = (z + dz) % 4
        last.append(
            remote(
                heads_out.at[zt], att_ref.at[:, pl.ds(z * 1024, 1024)],
                out_send.at[dz - 1], out_recv.at[dz - 1], device(x, y, zt, c),
            )
        )
        last[-1].start()
    last.append(pltpu.make_async_copy(heads_out.at[z], att_ref.at[:, pl.ds(z * 1024, 1024)], local_sem.at[6]))
    last[-1].start()
    for copy in returns:
        copy.wait()

    groups = [(axis, n) for n in (0, 3) for axis in range(3)]
    tiles = [
        (axis, n) for axis, first_tile in groups for n in range(first_tile, min(first_tile + 3, PARTS[axis][2] // 256))
    ]

    def fetch(t):
        axis, n = tiles[t]
        return pltpu.make_async_copy(
            cames[axis].at[:, :, 256 * n : 256 * (n + 1)], land.at[t % 2], land_sem.at[t % 2]
        )

    parts = []
    fetch(0).start()
    for t, (axis, n) in enumerate(tiles):
        if t + 1 < len(tiles):
            fetch(t + 1).start()
        fetch(t).wait()
        cut = slice(256 * n, 256 * (n + 1))
        for m in STEPS + (0,):
            both = jnp.dot(mixing[axis, m, :, 0:256], land[t % 2, m], preferred_element_type=F32)
            both = both + jnp.dot(mixing[axis, m, :, 256:512], land[t % 2, 4], preferred_element_type=F32)
            total = both[0:TOKENS] + both[TOKENS : 2 * TOKENS]
            if m == 0:
                at = PARTS[axis][1] + 256 * n
                own_sum[:, at : at + 256] = total
            else:
                lines[axis][TOKENS * m : TOKENS * (m + 1), cut] = total.astype(BF)
        if n in (2, PARTS[axis][2] // 256 - 1):
            half = slice(0, 768) if n == 2 else slice(768, PARTS[axis][2])
            for s, m in enumerate(STEPS):
                i = 3 * s + axis + (9 if n > 2 else 0)
                parts.append(
                    remote(
                        lines[axis].at[pl.ds(TOKENS * m, TOKENS), half], sums[axis].at[s, :, half],
                        sum_send.at[i], sum_recv.at[i], moved_back(line_offset(axis, m)),
                    )
                )
                parts[-1].start()
    for copy in last:
        copy.wait()
    for copy in parts:
        copy.wait()
    for axis, at, width in PARTS:
        total = own_sum[:, at : at + width]
        for s in range(3):
            total = total + sums[axis][s].astype(F32)
        work[0:TOKENS, at : at + width] = total.astype(BF)
    result = pltpu.make_async_copy(work.at[pl.ds(0, TOKENS)], mix_ref, local_sem.at[0])
    result.start()
    result.wait()


def body(
    queries, rotated_key_heads, stacked_value_heads, moe_rows, expert_ids, route_weights, w_gate, w_up, w_down
):
    hbm = pl.BlockSpec(memory_space=pl.ANY)
    dma = pltpu.SemaphoreType.DMA
    widths = [width for _, _, width in PARTS]
    results = pl.pallas_call(
        kernel,
        out_shape=(jax.ShapeDtypeStruct((SEQ, D), BF), jax.ShapeDtypeStruct((TOKENS, D), BF))
        + tuple(jax.ShapeDtypeStruct((5, 256, w), BF) for w in widths) * 2,
        in_specs=[hbm] * 9,
        out_specs=(hbm,) * 8,
        scratch_shapes=[pltpu.VMEM((4 * TOKENS, w), BF) for w in widths]
        + [pltpu.VMEM((5, 256, w), BF) for w in widths]
        + [
            pltpu.VMEM((8, TOKENS), jnp.int32),
            pltpu.VMEM((8, TOKENS), F32),
            pltpu.VMEM((16, TOKENS), F32),
            pltpu.VMEM((3, 4, 16, TOKENS), F32),
            pltpu.VMEM((3, 256, 4 * TOKENS), BF),
            pltpu.VMEM((16, 4, 2, SEQ, 256), BF),
            pltpu.VMEM((4, SEQ, 1024), BF),
            pltpu.VMEM((16, 128, 512), BF),
            pltpu.VMEM((4, SEQ, 1024), BF),
            pltpu.VMEM((640, D), BF),
            pltpu.VMEM((D, FFE), BF),
            pltpu.VMEM((D, FFE), BF),
            pltpu.VMEM((FFE, D), BF),
            pltpu.VMEM((640, FFE), BF),
            pltpu.VMEM((2, 5, 256, 256), BF),
            pltpu.VMEM((3, 4, 2 * TOKENS, 512), BF),
        ]
        + [pltpu.VMEM((3, TOKENS, w), BF) for w in widths]
        + [pltpu.VMEM((TOKENS, D), F32)]
        + [dma((n,)) for n in (93, 93, 9, 9, 9, 9, 9, 9, 15, 15, 16, 16, 3, 3, 10)]
        + [dma((n,)) for n in (1, 3, 93, 93, 18, 18, 2)],
        compiler_params=pltpu.CompilerParams(
            collective_id=0, has_side_effects=True, vmem_limit_bytes=62 * 2**20
        ),
        name="attend_and_mix",
    )(
        queries, rotated_key_heads, stacked_value_heads, moe_rows, expert_ids.T, route_weights.T,
        w_gate, w_up, w_down,
    )
    return results[0], results[1]


def solution(mesh):
    rows = P(("ctx", "exp"), None)
    cube = P(("ctx", "exp"), None, None)
    return jax.shard_map(
        body,
        mesh=mesh,
        in_specs=(rows,) * 6 + (cube,) * 3,
        out_specs=(rows, rows),
        check_vma=False,
    )
```

```python
import math

import jax
import jax.numpy as jnp
import numpy as np
from jax import lax
from jax.experimental import pallas as pl
from jax.experimental.pallas import tpu as pltpu
from jax.sharding import PartitionSpec as P

MESH = pl.DeviceIdType.MESH
BF = jnp.bfloat16
F32 = jnp.float32
D = 4096
FFE = 768
TOKENS = 128
SEQ = 64
PARTS = ((0, 0, 1536), (1, 1536, 1280), (2, 2816, 1280))
STEPS = (1, 3, 2)


def plane_offset(axis, i):
    d = [0, 0, 0]
    d[(axis + 1) % 3] = i // 4 % 4
    d[(axis + 2) % 3] = i % 4
    return tuple(d) + (i // 16,)


def line_offset(axis, m):
    d = [0, 0, 0, 0]
    d[axis] = m
    return tuple(d)


def shuffled(core):
    order = [(p, i) for p in range(3) for i in range(16 * core, 16 * core + 16)]
    np.random.RandomState(3 + core).shuffle(order)
    return [(int(p), int(i)) for p, i in order if i > 0]


PEERS = sorted({plane_offset(p, i) for p in range(3) for i in range(1, 32)})


def place():
    c = lax.axis_index("ctx")
    e = lax.axis_index("exp")
    return c % 4, c // 4, e // 2, e % 2


def device(x, y, z, c):
    return (y * 4 + x, z * 2 + c)


def moved(d):
    x, y, z, c = place()
    return device((x + d[0]) % 4, (y + d[1]) % 4, (z + d[2]) % 4, (c + d[3]) % 2)


def moved_back(d):
    return moved(((-d[0]) % 4, (-d[1]) % 4, (-d[2]) % 4, d[3]))


def greet_all():
    barrier = pltpu.get_barrier_semaphore()
    for d in PEERS:
        pl.semaphore_signal(barrier, inc=1, device_id=moved(d), device_id_type=MESH)


def await_all():
    pl.semaphore_wait(pltpu.get_barrier_semaphore(), len(PEERS))


def remote(src, dst, send, recv, target):
    return pltpu.make_async_remote_copy(
        src_ref=src, dst_ref=dst, send_sem=send, recv_sem=recv, device_id=target, device_id_type=MESH
    )


def owners(axis):
    x, y, z, c = place()
    i = lax.broadcasted_iota(jnp.int32, (32, TOKENS), 0)
    d = [0, 0, 0]
    d[(axis + 1) % 3] = i // 4 % 4
    d[(axis + 2) % 3] = i % 4
    chip = ((y + d[1]) % 4 * 4 + (x + d[0]) % 4) * 4 + (z + d[2]) % 4
    return (chip * 2 + (c + i // 16) % 2).astype(F32)


def ranks(ids, owner):
    named = jnp.zeros((32, TOKENS), F32)
    for k in range(8):
        named = named + jnp.where(ids[k : k + 1, :] == owner, 1.0, 0.0)
    shape = (TOKENS, TOKENS)
    before = lax.broadcasted_iota(jnp.int32, shape, 0) < lax.broadcasted_iota(jnp.int32, shape, 1)
    rank = jnp.dot(named.astype(BF), jnp.where(before, 1.0, 0.0).astype(BF), preferred_element_type=F32)
    return jnp.where(named > 0.5, rank, -1.0)


def spread(a):
    return jnp.broadcast_to(a[:, None, :], (32, 8, TOKENS)).reshape(256, TOKENS)


def line_index():
    return lax.broadcasted_iota(jnp.int32, (256, TOKENS), 0) % 8


def slot_masks(rank, m):
    row, line = spread(rank), line_index()
    early = row == line.astype(F32)
    late = (row == (8 + line % 2).astype(F32)) & (line // 2 == m)
    return early, late


def reorder(axis, forward):
    a = lax.broadcasted_iota(jnp.int32, (128, 128), 0 if forward else 1)
    b = lax.broadcasted_iota(jnp.int32, (128, 128), 1 if forward else 0)
    dx, dy, dz, s = a // 32, a // 8 % 4, a // 2 % 4, a % 2
    there = (dy * 4 + dz) * 8 + dx * 2 + s if axis == 0 else (dz * 4 + dx) * 8 + dy * 2 + s
    return jnp.where(there == b, 1.0, 0.0).astype(BF)


def kernel(
    q_ref, k_ref, v_ref, rows_ref, ids_ref, weight_ref, gate_ref, up_ref, down_ref,
    att_ref, mix_ref, recv_a, recv_b, recv_c, came_a, came_b, came_c, mid_a, mid_b, mid_c,
    line_a, line_b, line_c, pack_a, pack_b, pack_c, ids_here, weights_here, info, meta, late_hot,
    kv, queries, v_turned, heads_out, work, gate, up, down, hidden, land, mixing, sum_a, sum_b, sum_c, own_sum,
    send_sem, recv_sem, line_send, line_recv, meta_send, meta_recv, in_send, in_recv,
    kv_send, kv_recv, core_send, core_recv, out_send, out_recv, local_sem,
    load_sem, w_sem, back_send, back_recv, sum_send, sum_recv, land_sem,
    hop_send, hop_recv, stay_sem,
):
    x, y, z, c = place()
    ctx = y * 4 + x
    lines, packs, recvs = (line_a, line_b, line_c), (pack_a, pack_b, pack_c), (recv_a, recv_b, recv_c)
    cames, sums, mids = (came_a, came_b, came_c), (sum_a, sum_b, sum_c), (mid_a, mid_b, mid_c)
    greet_all()
    small = [
        pltpu.make_async_copy(ids_ref, ids_here, land_sem.at[0]),
        pltpu.make_async_copy(weight_ref, weights_here, land_sem.at[1]),
    ]
    for copy in small:
        copy.start()
    mine = [
        pltpu.make_async_copy(rows_ref.at[:, at : at + width], lines[axis].at[pl.ds(0, TOKENS)], local_sem.at[7 + axis])
        for axis, at, width in PARTS
    ]
    for copy in mine:
        copy.start()
    for copy in small:
        copy.wait()
    info[0:8, :] = ids_here[...].astype(F32)
    info[8:16, :] = weights_here[...]
    await_all()

    first = []
    for dz in range(4):
        zt = (z + dz) % 4
        for n, ref in enumerate((k_ref, v_ref)):
            there = ref.at[:, pl.ds(zt * 128, 128)]
            here = kv.at[ctx, z, c, :, pl.ds(128 * n, 128)]
            if dz == 0:
                first.append(pltpu.make_async_copy(there, here, local_sem.at[n]))
            else:
                i = (dz - 1) * 3 + n
                first.append(remote(there, here, in_send.at[i], in_recv.at[i], device(x, y, zt, c)))
            first[-1].start()

    along = {}
    for n, m in enumerate(STEPS):
        for axis, at, width in PARTS:
            target = moved(line_offset(axis, m))
            i = 3 * n + axis
            told = remote(info, meta.at[axis, m], meta_send.at[i], meta_recv.at[i], target)
            told.start()
            data = remote(
                rows_ref.at[:, at : at + width], lines[axis].at[pl.ds(TOKENS * m, TOKENS)],
                line_send.at[i], line_recv.at[i], target,
            )
            data.start()
            along[axis, m] = (told, data)

    asked = []
    for dz in range(4):
        zt = (z + dz) % 4
        there = q_ref.at[:, pl.ds(zt * 1024, 1024)]
        if dz == 0:
            asked.append(pltpu.make_async_copy(there, queries.at[z], local_sem.at[2]))
        else:
            i = (dz - 1) * 3 + 2
            asked.append(remote(there, queries.at[z], in_send.at[i], in_recv.at[i], device(x, y, zt, c)))
        asked[-1].start()

    for copy in first:
        copy.wait()
    for k in range(1, 16):

        @pl.when(ctx + k < 16)
        def _():
            there = ctx + k
            remote(
                kv.at[ctx, :, c], kv.at[ctx, :, c], kv_send.at[k - 1], kv_recv.at[k - 1], (there, z * 2 + c)
            ).start()

    weights = [
        pltpu.make_async_copy(gate_ref.at[0], gate, w_sem.at[0]),
        pltpu.make_async_copy(up_ref.at[0], up, w_sem.at[1]),
        pltpu.make_async_copy(down_ref.at[0], down, w_sem.at[2]),
    ]
    for copy in weights:
        copy.start()

    for m in (0,) + STEPS:
        for axis, at, width in PARTS:
            if m == 0:
                meta[axis, 0] = info[...]
                mine[axis].wait()
            else:
                for copy in along[axis, m]:
                    copy.wait()
            early, late = slot_masks(ranks(meta[axis, m], owners(axis)), m)
            hot = jnp.where(early, 1.0, 0.0).astype(BF)
            late_hot[axis, :, TOKENS * m : TOKENS * (m + 1)] = jnp.where(late, 1.0, 0.0).astype(BF)
            packs[axis][m] = jnp.dot(
                hot, lines[axis][TOKENS * m : TOKENS * (m + 1), :], preferred_element_type=F32
            ).astype(BF)
    for axis, at, width in PARTS:
        packs[axis][4] = jnp.dot(late_hot[axis], lines[axis][...], preferred_element_type=F32).astype(BF)

    hops = {}
    sends = ([], [])
    stays = []

    def hop(core):
        for d1 in STEPS:
            for axis in range(3):
                n = (axis * 2 + core) * 3 + d1 - 1
                hops[axis, core, d1] = remote(
                    packs[axis].at[:, pl.ds(8 * (16 * core + 4 * d1), 32)], mids[axis].at[core, d1 - 1],
                    hop_send.at[n], hop_recv.at[n], moved(line_offset((axis + 1) % 3, d1)),
                )
                hops[axis, core, d1].start()

    def leg(core, d1):
        for axis in range(3):
            if d1 > 0:
                hops[axis, core, d1].wait_recv()
            for d2 in STEPS + (0,):
                i = 16 * core + 4 * d1 + d2
                n = 31 * axis + i - 1
                here = pl.ds(8 * i, 8)
                from_ref = packs[axis].at[:, here] if d1 == 0 else mids[axis].at[core, d1 - 1, :, pl.ds(8 * d2, 8)]
                if core == 0 and d2 == 0:
                    stays.append(pltpu.make_async_copy(from_ref, recvs[axis].at[:, here], stay_sem.at[4 * axis + d1]))
                    stays[-1].start()
                else:
                    target = moved(line_offset((axis + 2) % 3, d2)[:3] + (core,))
                    sends[core].append(
                        remote(from_ref, recvs[axis].at[:, here], send_sem.at[n], recv_sem.at[n], target)
                    )
                    sends[core][-1].start()

    hop(0)
    leg(0, 0)
    hop(1)

    for copy in asked:
        copy.wait()
    for k in range(1, 16):
        copy = remote(
            kv.at[ctx, :, c], kv.at[ctx, :, c], kv_send.at[k - 1], kv_recv.at[k - 1], (ctx, z * 2 + c)
        )

        @pl.when(ctx >= k)
        def _():
            copy.wait_recv()

        @pl.when(ctx + k < 16)
        def _():
            copy.wait_send()

    def core_copy(j):
        return remote(
            kv.at[j, :, c], kv.at[j, :, c], core_send.at[j], core_recv.at[j], device(x, y, z, 1 - c)
        )

    def core_start(j, carry):
        core_copy(j).start()
        return carry

    def core_wait(j, carry):
        core_copy(j).wait()
        return carry

    lax.fori_loop(0, ctx + 1, core_start, 0)
    lax.fori_loop(0, ctx + 1, core_wait, 0)

    def turn(j, carry):
        block = kv[j].reshape(512, 256)
        v_turned[j] = block[:, 128:256].astype(F32).T.astype(BF)
        return carry

    lax.fori_loop(0, ctx + 1, turn, 0)
    factor = math.log2(math.e) / math.sqrt(128.0)
    column = lax.broadcasted_iota(jnp.int32, (512, 256), 1)
    allowed = lax.broadcasted_iota(jnp.int32, (512, 256), 0) <= (column // 64 * 2 + c) * 64 + column % 64

    def head(h, carry):
        cut = pl.ds(pl.multiple_of(h * 128, 128), 128)
        q = queries[:, :, cut].reshape(256, 128)

        def step(j, state, masked):
            row_max, row_sum, total = state
            key = kv[j].reshape(512, 256)[:, 0:128]
            score = lax.dot_general(key, q, (((1,), (1,)), ((), ())), preferred_element_type=F32) * factor
            if masked:
                score = jnp.where(allowed, score, -1e30)
            new_max = jnp.maximum(row_max, jnp.max(score, axis=0, keepdims=True))
            prob = jnp.exp2(score - new_max)
            old = jnp.exp2(row_max - new_max)
            row_sum = row_sum * old + jnp.sum(prob, axis=0, keepdims=True)
            total = total * old + jnp.dot(v_turned[j], prob.astype(BF), preferred_element_type=F32)
            return (new_max, row_sum, total)

        state = (
            jnp.full((1, 256), -1e30, F32),
            jnp.zeros((1, 256), F32),
            jnp.zeros((128, 256), F32),
        )
        state = step(ctx, state, True)
        state = lax.fori_loop(0, ctx, lambda j, s: step(j, s, False), state)
        result = (state[2] / state[1]).T
        heads_out[:, :, cut] = result.reshape(4, 64, 128).astype(BF)
        return carry

    for h, d1 in enumerate(STEPS):
        lax.fori_loop(h, h + 1, head, 0)
        leg(0, d1)
    leg(1, 0)
    lax.fori_loop(3, 4, head, 0)
    for d1 in STEPS:
        leg(1, d1)

    def load(core):
        at = 128 * core
        for dx in range(4):
            pltpu.make_async_copy(
                recv_a.at[dx, pl.ds(at, 128)], work.at[pl.ds(128 * dx, 128), 0:1536], load_sem.at[0]
            ).start()
        pltpu.make_async_copy(recv_a.at[4, pl.ds(at, 128)], work.at[pl.ds(512, 128), 0:1536], load_sem.at[0]).start()
        pltpu.make_async_copy(recv_b.at[4, pl.ds(at, 128)], work.at[pl.ds(512, 128), 1536:2816], load_sem.at[0]).start()

        def piece(n, carry):
            pltpu.make_async_copy(
                recv_b.at[n // 4 % 4, pl.ds(pl.multiple_of(at + (n % 4 * 4 + n // 16) * 8, 8), 8)],
                work.at[pl.ds(pl.multiple_of(8 * n, 8), 8), 1536:2816],
                load_sem.at[0],
            ).start()
            pltpu.make_async_copy(
                recv_c.at[n % 4, pl.ds(pl.multiple_of(at + n // 4 * 8, 8), 8)],
                work.at[pl.ds(pl.multiple_of(8 * n, 8), 8), 2816:4096],
                load_sem.at[0],
            ).start()
            return carry

        lax.fori_loop(0, 64, piece, 0)
        pltpu.make_async_copy(recv_c.at[4, pl.ds(at, 128)], work.at[pl.ds(512, 128), 2816:4096], load_sem.at[0]).start()

    returns = []
    for core in range(2):
        for copy in sends[core]:
            copy.wait_recv()
        if core == 0:
            for copy in stays:
                copy.wait()
        load(core)
        pltpu.make_async_copy(work, work, load_sem.at[0]).wait()
        if core == 0:
            weights[0].wait()
            weights[1].wait()
        for axis, at, width in PARTS[:2]:
            work[512:640, at : at + width] = jnp.dot(
                reorder(axis, True), work[512:640, at : at + width], preferred_element_type=F32
            ).astype(BF)

        def inner(n, carry):
            cut = pl.ds(pl.multiple_of(n * 256, 256), 256)
            a = jnp.dot(work[...], gate[:, cut], preferred_element_type=F32)
            b = jnp.dot(work[...], up[:, cut], preferred_element_type=F32)
            hidden[:, cut] = (a / (1.0 + jnp.exp(-a)) * b).astype(BF)
            return carry

        lax.fori_loop(0, 3, inner, 0)
        if core == 0:
            weights[2].wait()
        for copy in [hops[axis, core, d1] for axis in range(3) for d1 in STEPS] + sends[core]:
            copy.wait_send()
        for axis, at, width in PARTS:
            ref = packs[axis]

            def outer(n, carry):
                cut = pl.ds(pl.multiple_of(n * 256, 256), 256)
                from_cut = pl.ds(pl.multiple_of(at + n * 256, 256), 256)
                value = jnp.dot(hidden[...], down[:, from_cut], preferred_element_type=F32)
                row = 128 * core
                if axis == 0:
                    for dx in range(4):
                        ref[dx, row : row + 128, cut] = value[128 * dx : 128 * (dx + 1)].astype(BF)
                elif axis == 1:
                    for n2 in range(64):
                        to = row + (n2 % 4 * 4 + n2 // 16) * 8
                        ref[n2 // 4 % 4, to : to + 8, cut] = value[8 * n2 : 8 * (n2 + 1)].astype(BF)
                else:
                    for n2 in range(64):
                        to = row + n2 // 4 * 8
                        ref[n2 % 4, to : to + 8, cut] = value[8 * n2 : 8 * (n2 + 1)].astype(BF)
                late = value[512:640].astype(BF)
                if axis < 2:
                    late = jnp.dot(reorder(axis, False), late, preferred_element_type=F32).astype(BF)
                ref[4, row : row + 128, cut] = late
                return carry

            lax.fori_loop(0, width // 256, outer, 0)
        for axis, i in shuffled(core):
            cut = pl.ds(8 * i, 8)
            n = 31 * axis + i - 1
            returns.append(
                remote(
                    packs[axis].at[:, cut], cames[axis].at[:, cut],
                    back_send.at[n], back_recv.at[n], moved_back(plane_offset(axis, i)),
                )
            )
            returns[-1].start()
        if core == 0:
            for axis in range(3):
                cut = pl.ds(0, 8)
                returns.append(
                    pltpu.make_async_copy(packs[axis].at[:, cut], cames[axis].at[:, cut], local_sem.at[3 + axis])
                )
                returns[-1].start()

    for axis, at, width in PARTS:
        for m in range(4):
            early, late = slot_masks(ranks(meta[axis, m], owners(axis)), m)
            value = jnp.zeros((32, TOKENS), F32)
            for k in range(8):
                value = value + jnp.where(
                    meta[axis, m, k : k + 1, :] == owners(axis), meta[axis, m, 8 + k : 9 + k, :], 0.0
                )
            value = spread(value)
            for n, mask in enumerate((early, late)):
                turned = jnp.where(mask, value, 0.0).T
                high = turned.astype(BF)
                mixing[axis, m, 0:TOKENS, 256 * n : 256 * (n + 1)] = high
                mixing[axis, m, TOKENS : 2 * TOKENS, 256 * n : 256 * (n + 1)] = (turned - high.astype(F32)).astype(BF)
    lax.fori_loop(4, 8, head, 0)
    last = []
    for dz in range(1, 4):
        zt = (z + dz) % 4
        last.append(
            remote(
                heads_out.at[zt], att_ref.at[:, pl.ds(z * 1024, 1024)],
                out_send.at[dz - 1], out_recv.at[dz - 1], device(x, y, zt, c),
            )
        )
        last[-1].start()
    last.append(pltpu.make_async_copy(heads_out.at[z], att_ref.at[:, pl.ds(z * 1024, 1024)], local_sem.at[6]))
    last[-1].start()
    for copy in returns:
        copy.wait()

    groups = [(axis, n) for n in (0, 3) for axis in range(3)]
    tiles = [
        (axis, n) for axis, first_tile in groups for n in range(first_tile, min(first_tile + 3, PARTS[axis][2] // 256))
    ]

    def fetch(t):
        axis, n = tiles[t]
        return pltpu.make_async_copy(
            cames[axis].at[:, :, 256 * n : 256 * (n + 1)], land.at[t % 2], land_sem.at[t % 2]
        )

    parts = []
    fetch(0).start()
    for t, (axis, n) in enumerate(tiles):
        if t + 1 < len(tiles):
            fetch(t + 1).start()
        fetch(t).wait()
        cut = slice(256 * n, 256 * (n + 1))
        for m in STEPS + (0,):
            both = jnp.dot(mixing[axis, m, :, 0:256], land[t % 2, m], preferred_element_type=F32)
            both = both + jnp.dot(mixing[axis, m, :, 256:512], land[t % 2, 4], preferred_element_type=F32)
            total = both[0:TOKENS] + both[TOKENS : 2 * TOKENS]
            if m == 0:
                at = PARTS[axis][1] + 256 * n
                own_sum[:, at : at + 256] = total
            else:
                lines[axis][TOKENS * m : TOKENS * (m + 1), cut] = total.astype(BF)
        if n in (2, PARTS[axis][2] // 256 - 1):
            half = slice(0, 768) if n == 2 else slice(768, PARTS[axis][2])
            for s, m in enumerate(STEPS):
                i = 3 * s + axis + (9 if n > 2 else 0)
                parts.append(
                    remote(
                        lines[axis].at[pl.ds(TOKENS * m, TOKENS), half], sums[axis].at[s, :, half],
                        sum_send.at[i], sum_recv.at[i], moved_back(line_offset(axis, m)),
                    )
                )
                parts[-1].start()
    for copy in last:
        copy.wait()
    for copy in parts:
        copy.wait()
    for axis, at, width in PARTS:
        total = own_sum[:, at : at + width]
        for s in range(3):
            total = total + sums[axis][s].astype(F32)
        work[0:TOKENS, at : at + width] = total.astype(BF)
    result = pltpu.make_async_copy(work.at[pl.ds(0, TOKENS)], mix_ref, local_sem.at[0])
    result.start()
    result.wait()


def body(
    queries, rotated_key_heads, stacked_value_heads, moe_rows, expert_ids, route_weights, w_gate, w_up, w_down
):
    hbm = pl.BlockSpec(memory_space=pl.ANY)
    dma = pltpu.SemaphoreType.DMA
    widths = [width for _, _, width in PARTS]
    results = pl.pallas_call(
        kernel,
        out_shape=(jax.ShapeDtypeStruct((SEQ, D), BF), jax.ShapeDtypeStruct((TOKENS, D), BF))
        + tuple(jax.ShapeDtypeStruct((5, 256, w), BF) for w in widths) * 2
        + tuple(jax.ShapeDtypeStruct((2, 3, 5, 32, w), BF) for w in widths),
        in_specs=[hbm] * 9,
        out_specs=(hbm,) * 11,
        scratch_shapes=[pltpu.VMEM((4 * TOKENS, w), BF) for w in widths]
        + [pltpu.VMEM((5, 256, w), BF) for w in widths]
        + [
            pltpu.VMEM((8, TOKENS), jnp.int32),
            pltpu.VMEM((8, TOKENS), F32),
            pltpu.VMEM((16, TOKENS), F32),
            pltpu.VMEM((3, 4, 16, TOKENS), F32),
            pltpu.VMEM((3, 256, 4 * TOKENS), BF),
            pltpu.VMEM((16, 4, 2, SEQ, 256), BF),
            pltpu.VMEM((4, SEQ, 1024), BF),
            pltpu.VMEM((16, 128, 512), BF),
            pltpu.VMEM((4, SEQ, 1024), BF),
            pltpu.VMEM((640, D), BF),
            pltpu.VMEM((D, FFE), BF),
            pltpu.VMEM((D, FFE), BF),
            pltpu.VMEM((FFE, D), BF),
            pltpu.VMEM((640, FFE), BF),
            pltpu.VMEM((2, 5, 256, 256), BF),
            pltpu.VMEM((3, 4, 2 * TOKENS, 512), BF),
        ]
        + [pltpu.VMEM((3, TOKENS, w), BF) for w in widths]
        + [pltpu.VMEM((TOKENS, D), F32)]
        + [dma((n,)) for n in (93, 93, 9, 9, 9, 9, 9, 9, 15, 15, 16, 16, 3, 3, 10)]
        + [dma((n,)) for n in (1, 3, 93, 93, 18, 18, 2, 18, 18, 12)],
        compiler_params=pltpu.CompilerParams(
            collective_id=0, has_side_effects=True, vmem_limit_bytes=62 * 2**20
        ),
        name="attend_and_mix",
    )(
        queries, rotated_key_heads, stacked_value_heads, moe_rows, expert_ids.T, route_weights.T,
        w_gate, w_up, w_down,
    )
    return results[0], results[1]


def solution(mesh):
    rows = P(("ctx", "exp"), None)
    cube = P(("ctx", "exp"), None, None)
    return jax.shard_map(
        body,
        mesh=mesh,
        in_specs=(rows,) * 6 + (cube,) * 3,
        out_specs=(rows, rows),
        check_vma=False,
    )
```

```python
import math

import jax
import jax.numpy as jnp
import numpy as np
from jax import lax
from jax.experimental import pallas as pl
from jax.experimental.pallas import tpu as pltpu
from jax.sharding import PartitionSpec as P

MESH = pl.DeviceIdType.MESH
BF = jnp.bfloat16
F32 = jnp.float32
D = 4096
FFE = 768
TOKENS = 128
SEQ = 64
PARTS = ((0, 0, 1536), (1, 1536, 1280), (2, 2816, 1280))
STEPS = (1, 3, 2)


def plane_offset(axis, i):
    d = [0, 0, 0]
    d[(axis + 1) % 3] = i // 4 % 4
    d[(axis + 2) % 3] = i % 4
    return tuple(d) + (i // 16,)


def line_offset(axis, m):
    d = [0, 0, 0, 0]
    d[axis] = m
    return tuple(d)


PEERS = sorted({plane_offset(p, i) for p in range(3) for i in range(1, 32)})


def place():
    c = lax.axis_index("ctx")
    e = lax.axis_index("exp")
    return c % 4, c // 4, e // 2, e % 2


def device(x, y, z, c):
    return (y * 4 + x, z * 2 + c)


def moved(d):
    x, y, z, c = place()
    return device((x + d[0]) % 4, (y + d[1]) % 4, (z + d[2]) % 4, (c + d[3]) % 2)


def moved_back(d):
    return moved(((-d[0]) % 4, (-d[1]) % 4, (-d[2]) % 4, d[3]))


def greet_all():
    barrier = pltpu.get_barrier_semaphore()
    for d in PEERS:
        pl.semaphore_signal(barrier, inc=1, device_id=moved(d), device_id_type=MESH)


def await_all():
    pl.semaphore_wait(pltpu.get_barrier_semaphore(), len(PEERS))


def remote(src, dst, send, recv, target):
    return pltpu.make_async_remote_copy(
        src_ref=src, dst_ref=dst, send_sem=send, recv_sem=recv, device_id=target, device_id_type=MESH
    )


def owners(axis):
    x, y, z, c = place()
    i = lax.broadcasted_iota(jnp.int32, (32, TOKENS), 0)
    d = [0, 0, 0]
    d[(axis + 1) % 3] = i // 4 % 4
    d[(axis + 2) % 3] = i % 4
    chip = ((y + d[1]) % 4 * 4 + (x + d[0]) % 4) * 4 + (z + d[2]) % 4
    return (chip * 2 + (c + i // 16) % 2).astype(F32)


def ranks(ids, owner):
    named = jnp.zeros((32, TOKENS), F32)
    for k in range(8):
        named = named + jnp.where(ids[k : k + 1, :] == owner, 1.0, 0.0)
    shape = (TOKENS, TOKENS)
    before = lax.broadcasted_iota(jnp.int32, shape, 0) < lax.broadcasted_iota(jnp.int32, shape, 1)
    rank = jnp.dot(named.astype(BF), jnp.where(before, 1.0, 0.0).astype(BF), preferred_element_type=F32)
    return jnp.where(named > 0.5, rank, -1.0)


def spread(a):
    return jnp.broadcast_to(a[:, None, :], (32, 8, TOKENS)).reshape(256, TOKENS)


def line_index():
    return lax.broadcasted_iota(jnp.int32, (256, TOKENS), 0) % 8


def slot_masks(rank, m):
    row, line = spread(rank), line_index()
    early = row == line.astype(F32)
    late = (row == (8 + line % 2).astype(F32)) & (line // 2 == m)
    return early, late


def reorder(axis, forward):
    a = lax.broadcasted_iota(jnp.int32, (128, 128), 0 if forward else 1)
    b = lax.broadcasted_iota(jnp.int32, (128, 128), 1 if forward else 0)
    dx, dy, dz, s = a // 32, a // 8 % 4, a // 2 % 4, a % 2
    there = (dy * 4 + dz) * 8 + dx * 2 + s if axis == 0 else (dz * 4 + dx) * 8 + dy * 2 + s
    return jnp.where(there == b, 1.0, 0.0).astype(BF)


def kernel(
    q_ref, k_ref, v_ref, rows_ref, ids_ref, weight_ref, gate_ref, up_ref, down_ref,
    att_ref, mix_ref, recv_a, recv_b, recv_c, came_a, came_b, came_c, mid_a, mid_b, mid_c,
    back_mid_a, back_mid_b, back_mid_c,
    line_a, line_b, line_c, pack_a, pack_b, pack_c, ids_here, weights_here, info, meta, late_hot,
    kv, queries, v_turned, heads_out, work, gate, up, down, hidden, land, mixing, sum_a, sum_b, sum_c, own_sum,
    send_sem, recv_sem, line_send, line_recv, meta_send, meta_recv, in_send, in_recv,
    kv_send, kv_recv, core_send, core_recv, out_send, out_recv, local_sem,
    load_sem, w_sem, back_send, back_recv, sum_send, sum_recv, land_sem,
    hop_send, hop_recv, stay_sem, back_hop_send, back_hop_recv,
):
    x, y, z, c = place()
    ctx = y * 4 + x
    lines, packs, recvs = (line_a, line_b, line_c), (pack_a, pack_b, pack_c), (recv_a, recv_b, recv_c)
    cames, sums, mids = (came_a, came_b, came_c), (sum_a, sum_b, sum_c), (mid_a, mid_b, mid_c)
    back_mids = (back_mid_a, back_mid_b, back_mid_c)
    greet_all()
    small = [
        pltpu.make_async_copy(ids_ref, ids_here, land_sem.at[0]),
        pltpu.make_async_copy(weight_ref, weights_here, land_sem.at[1]),
    ]
    for copy in small:
        copy.start()
    mine = [
        pltpu.make_async_copy(rows_ref.at[:, at : at + width], lines[axis].at[pl.ds(0, TOKENS)], local_sem.at[7 + axis])
        for axis, at, width in PARTS
    ]
    for copy in mine:
        copy.start()
    for copy in small:
        copy.wait()
    info[0:8, :] = ids_here[...].astype(F32)
    info[8:16, :] = weights_here[...]
    await_all()

    first = []
    for dz in range(4):
        zt = (z + dz) % 4
        for n, ref in enumerate((k_ref, v_ref)):
            there = ref.at[:, pl.ds(zt * 128, 128)]
            here = kv.at[ctx, z, c, :, pl.ds(128 * n, 128)]
            if dz == 0:
                first.append(pltpu.make_async_copy(there, here, local_sem.at[n]))
            else:
                i = (dz - 1) * 3 + n
                first.append(remote(there, here, in_send.at[i], in_recv.at[i], device(x, y, zt, c)))
            first[-1].start()

    along = {}
    for n, m in enumerate(STEPS):
        for axis, at, width in PARTS:
            target = moved(line_offset(axis, m))
            i = 3 * n + axis
            told = remote(info, meta.at[axis, m], meta_send.at[i], meta_recv.at[i], target)
            told.start()
            data = remote(
                rows_ref.at[:, at : at + width], lines[axis].at[pl.ds(TOKENS * m, TOKENS)],
                line_send.at[i], line_recv.at[i], target,
            )
            data.start()
            along[axis, m] = (told, data)

    asked = []
    for dz in range(4):
        zt = (z + dz) % 4
        there = q_ref.at[:, pl.ds(zt * 1024, 1024)]
        if dz == 0:
            asked.append(pltpu.make_async_copy(there, queries.at[z], local_sem.at[2]))
        else:
            i = (dz - 1) * 3 + 2
            asked.append(remote(there, queries.at[z], in_send.at[i], in_recv.at[i], device(x, y, zt, c)))
        asked[-1].start()

    for copy in first:
        copy.wait()
    for k in range(1, 16):

        @pl.when(ctx + k < 16)
        def _():
            there = ctx + k
            remote(
                kv.at[ctx, :, c], kv.at[ctx, :, c], kv_send.at[k - 1], kv_recv.at[k - 1], (there, z * 2 + c)
            ).start()

    weights = [
        pltpu.make_async_copy(gate_ref.at[0], gate, w_sem.at[0]),
        pltpu.make_async_copy(up_ref.at[0], up, w_sem.at[1]),
        pltpu.make_async_copy(down_ref.at[0], down, w_sem.at[2]),
    ]
    for copy in weights:
        copy.start()

    for m in (0,) + STEPS:
        for axis, at, width in PARTS:
            if m == 0:
                meta[axis, 0] = info[...]
                mine[axis].wait()
            else:
                for copy in along[axis, m]:
                    copy.wait()
            early, late = slot_masks(ranks(meta[axis, m], owners(axis)), m)
            hot = jnp.where(early, 1.0, 0.0).astype(BF)
            late_hot[axis, :, TOKENS * m : TOKENS * (m + 1)] = jnp.where(late, 1.0, 0.0).astype(BF)
            packs[axis][m] = jnp.dot(
                hot, lines[axis][TOKENS * m : TOKENS * (m + 1), :], preferred_element_type=F32
            ).astype(BF)
    for axis, at, width in PARTS:
        packs[axis][4] = jnp.dot(late_hot[axis], lines[axis][...], preferred_element_type=F32).astype(BF)

    hops = {}
    sends = ([], [])
    stays = []

    def hop(core):
        for d1 in STEPS:
            for axis in range(3):
                n = (axis * 2 + core) * 3 + d1 - 1
                hops[axis, core, d1] = remote(
                    packs[axis].at[:, pl.ds(8 * (16 * core + 4 * d1), 32)], mids[axis].at[core, d1 - 1],
                    hop_send.at[n], hop_recv.at[n], moved(line_offset((axis + 1) % 3, d1)),
                )
                hops[axis, core, d1].start()

    def leg(core, d1):
        for axis in range(3):
            if d1 > 0:
                hops[axis, core, d1].wait_recv()
            for d2 in STEPS + (0,):
                i = 16 * core + 4 * d1 + d2
                n = 31 * axis + i - 1
                here = pl.ds(8 * i, 8)
                from_ref = packs[axis].at[:, here] if d1 == 0 else mids[axis].at[core, d1 - 1, :, pl.ds(8 * d2, 8)]
                if core == 0 and d2 == 0:
                    stays.append(pltpu.make_async_copy(from_ref, recvs[axis].at[:, here], stay_sem.at[4 * axis + d1]))
                    stays[-1].start()
                else:
                    target = moved(line_offset((axis + 2) % 3, d2)[:3] + (core,))
                    sends[core].append(
                        remote(from_ref, recvs[axis].at[:, here], send_sem.at[n], recv_sem.at[n], target)
                    )
                    sends[core][-1].start()

    hop(0)
    leg(0, 0)
    hop(1)

    for copy in asked:
        copy.wait()
    for k in range(1, 16):
        copy = remote(
            kv.at[ctx, :, c], kv.at[ctx, :, c], kv_send.at[k - 1], kv_recv.at[k - 1], (ctx, z * 2 + c)
        )

        @pl.when(ctx >= k)
        def _():
            copy.wait_recv()

        @pl.when(ctx + k < 16)
        def _():
            copy.wait_send()

    def core_copy(j):
        return remote(
            kv.at[j, :, c], kv.at[j, :, c], core_send.at[j], core_recv.at[j], device(x, y, z, 1 - c)
        )

    def core_start(j, carry):
        core_copy(j).start()
        return carry

    def core_wait(j, carry):
        core_copy(j).wait()
        return carry

    lax.fori_loop(0, ctx + 1, core_start, 0)
    lax.fori_loop(0, ctx + 1, core_wait, 0)

    def turn(j, carry):
        block = kv[j].reshape(512, 256)
        v_turned[j] = block[:, 128:256].astype(F32).T.astype(BF)
        return carry

    lax.fori_loop(0, ctx + 1, turn, 0)
    factor = math.log2(math.e) / math.sqrt(128.0)
    column = lax.broadcasted_iota(jnp.int32, (512, 256), 1)
    allowed = lax.broadcasted_iota(jnp.int32, (512, 256), 0) <= (column // 64 * 2 + c) * 64 + column % 64

    def head(h, carry):
        cut = pl.ds(pl.multiple_of(h * 128, 128), 128)
        q = queries[:, :, cut].reshape(256, 128)

        def step(j, state, masked):
            row_max, row_sum, total = state
            key = kv[j].reshape(512, 256)[:, 0:128]
            score = lax.dot_general(key, q, (((1,), (1,)), ((), ())), preferred_element_type=F32) * factor
            if masked:
                score = jnp.where(allowed, score, -1e30)
            new_max = jnp.maximum(row_max, jnp.max(score, axis=0, keepdims=True))
            prob = jnp.exp2(score - new_max)
            old = jnp.exp2(row_max - new_max)
            row_sum = row_sum * old + jnp.sum(prob, axis=0, keepdims=True)
            total = total * old + jnp.dot(v_turned[j], prob.astype(BF), preferred_element_type=F32)
            return (new_max, row_sum, total)

        state = (
            jnp.full((1, 256), -1e30, F32),
            jnp.zeros((1, 256), F32),
            jnp.zeros((128, 256), F32),
        )
        state = step(ctx, state, True)
        state = lax.fori_loop(0, ctx, lambda j, s: step(j, s, False), state)
        result = (state[2] / state[1]).T
        heads_out[:, :, cut] = result.reshape(4, 64, 128).astype(BF)
        return carry

    for h, d1 in enumerate(STEPS):
        lax.fori_loop(h, h + 1, head, 0)
        leg(0, d1)
    leg(1, 0)
    lax.fori_loop(3, 5, head, 0)
    for d1 in STEPS:
        leg(1, d1)

    def load(core):
        at = 128 * core
        for dx in range(4):
            pltpu.make_async_copy(
                recv_a.at[dx, pl.ds(at, 128)], work.at[pl.ds(128 * dx, 128), 0:1536], load_sem.at[0]
            ).start()
        pltpu.make_async_copy(recv_a.at[4, pl.ds(at, 128)], work.at[pl.ds(512, 128), 0:1536], load_sem.at[0]).start()
        pltpu.make_async_copy(recv_b.at[4, pl.ds(at, 128)], work.at[pl.ds(512, 128), 1536:2816], load_sem.at[0]).start()

        def piece(n, carry):
            pltpu.make_async_copy(
                recv_b.at[n // 4 % 4, pl.ds(pl.multiple_of(at + (n % 4 * 4 + n // 16) * 8, 8), 8)],
                work.at[pl.ds(pl.multiple_of(8 * n, 8), 8), 1536:2816],
                load_sem.at[0],
            ).start()
            pltpu.make_async_copy(
                recv_c.at[n % 4, pl.ds(pl.multiple_of(at + n // 4 * 8, 8), 8)],
                work.at[pl.ds(pl.multiple_of(8 * n, 8), 8), 2816:4096],
                load_sem.at[0],
            ).start()
            return carry

        lax.fori_loop(0, 64, piece, 0)
        pltpu.make_async_copy(recv_c.at[4, pl.ds(at, 128)], work.at[pl.ds(512, 128), 2816:4096], load_sem.at[0]).start()

    legs = {}
    back_hops = []

    def back_leg(core):
        for d1 in STEPS + (0,):
            for d2 in STEPS + (0,):
                for axis in range(3):
                    i = 16 * core + 4 * d1 + d2
                    n = 31 * axis + i - 1
                    here = packs[axis].at[:, pl.ds(8 * i, 8)]
                    there = (
                        cames[axis].at[:, pl.ds(8 * i, 8)]
                        if d1 == 0
                        else back_mids[axis].at[core, d1 - 1, :, pl.ds(8 * d2, 8)]
                    )
                    if core == 0 and d2 == 0:
                        copy = pltpu.make_async_copy(here, there, stay_sem.at[4 * axis + d1])
                    else:
                        target = moved_back(line_offset((axis + 2) % 3, d2)[:3] + (core,))
                        copy = remote(here, there, back_send.at[n], back_recv.at[n], target)
                    copy.start()
                    legs[axis, core, d1, d2] = copy

    def back_hop(core, d1):
        for axis in range(3):
            for d2 in range(4):
                copy = legs[axis, core, d1, d2]
                if core == 0 and d2 == 0:
                    copy.wait()
                else:
                    copy.wait_recv()
            n = (axis * 2 + core) * 3 + d1 - 1
            back_hops.append(
                remote(
                    back_mids[axis].at[core, d1 - 1], cames[axis].at[:, pl.ds(8 * (16 * core + 4 * d1), 32)],
                    back_hop_send.at[n], back_hop_recv.at[n], moved_back(line_offset((axis + 1) % 3, d1)),
                )
            )
            back_hops[-1].start()

    for core in range(2):
        for copy in sends[core]:
            copy.wait_recv()
        if core == 0:
            for copy in stays:
                copy.wait()
        load(core)
        pltpu.make_async_copy(work, work, load_sem.at[0]).wait()
        if core == 0:
            weights[0].wait()
            weights[1].wait()
        for axis, at, width in PARTS[:2]:
            work[512:640, at : at + width] = jnp.dot(
                reorder(axis, True), work[512:640, at : at + width], preferred_element_type=F32
            ).astype(BF)

        def inner(n, carry):
            cut = pl.ds(pl.multiple_of(n * 256, 256), 256)
            a = jnp.dot(work[...], gate[:, cut], preferred_element_type=F32)
            b = jnp.dot(work[...], up[:, cut], preferred_element_type=F32)
            hidden[:, cut] = (a / (1.0 + jnp.exp(-a)) * b).astype(BF)
            return carry

        lax.fori_loop(0, 3, inner, 0)
        if core == 1:
            for d1 in STEPS:
                back_hop(0, d1)
        if core == 0:
            weights[2].wait()
        for copy in [hops[axis, core, d1] for axis in range(3) for d1 in STEPS] + sends[core]:
            copy.wait_send()
        for axis, at, width in PARTS:
            ref = packs[axis]

            def outer(n, carry):
                cut = pl.ds(pl.multiple_of(n * 256, 256), 256)
                from_cut = pl.ds(pl.multiple_of(at + n * 256, 256), 256)
                value = jnp.dot(hidden[...], down[:, from_cut], preferred_element_type=F32)
                row = 128 * core
                if axis == 0:
                    for dx in range(4):
                        ref[dx, row : row + 128, cut] = value[128 * dx : 128 * (dx + 1)].astype(BF)
                elif axis == 1:
                    for n2 in range(64):
                        to = row + (n2 % 4 * 4 + n2 // 16) * 8
                        ref[n2 // 4 % 4, to : to + 8, cut] = value[8 * n2 : 8 * (n2 + 1)].astype(BF)
                else:
                    for n2 in range(64):
                        to = row + n2 // 4 * 8
                        ref[n2 % 4, to : to + 8, cut] = value[8 * n2 : 8 * (n2 + 1)].astype(BF)
                late = value[512:640].astype(BF)
                if axis < 2:
                    late = jnp.dot(reorder(axis, False), late, preferred_element_type=F32).astype(BF)
                ref[4, row : row + 128, cut] = late
                return carry

            lax.fori_loop(0, width // 256, outer, 0)
        back_leg(core)

    for axis, at, width in PARTS:
        for m in range(4):
            early, late = slot_masks(ranks(meta[axis, m], owners(axis)), m)
            value = jnp.zeros((32, TOKENS), F32)
            for k in range(8):
                value = value + jnp.where(
                    meta[axis, m, k : k + 1, :] == owners(axis), meta[axis, m, 8 + k : 9 + k, :], 0.0
                )
            value = spread(value)
            for n, mask in enumerate((early, late)):
                turned = jnp.where(mask, value, 0.0).T
                high = turned.astype(BF)
                mixing[axis, m, 0:TOKENS, 256 * n : 256 * (n + 1)] = high
                mixing[axis, m, TOKENS : 2 * TOKENS, 256 * n : 256 * (n + 1)] = (turned - high.astype(F32)).astype(BF)
    lax.fori_loop(5, 7, head, 0)
    for d1 in STEPS:
        back_hop(1, d1)
    lax.fori_loop(7, 8, head, 0)
    last = []
    for dz in range(1, 4):
        zt = (z + dz) % 4
        last.append(
            remote(
                heads_out.at[zt], att_ref.at[:, pl.ds(z * 1024, 1024)],
                out_send.at[dz - 1], out_recv.at[dz - 1], device(x, y, zt, c),
            )
        )
        last[-1].start()
    last.append(pltpu.make_async_copy(heads_out.at[z], att_ref.at[:, pl.ds(z * 1024, 1024)], local_sem.at[6]))
    last[-1].start()
    for (axis, core, d1, d2), copy in legs.items():
        if core == 0 and d2 == 0:
            if d1 == 0:
                copy.wait()
        else:
            copy.wait_send()
            if d1 == 0:
                copy.wait_recv()
    for copy in back_hops:
        copy.wait()

    groups = [(axis, n) for n in (0, 3) for axis in range(3)]
    tiles = [
        (axis, n) for axis, first_tile in groups for n in range(first_tile, min(first_tile + 3, PARTS[axis][2] // 256))
    ]

    def fetch(t):
        axis, n = tiles[t]
        return pltpu.make_async_copy(
            cames[axis].at[:, :, 256 * n : 256 * (n + 1)], land.at[t % 2], land_sem.at[t % 2]
        )

    parts = []
    fetch(0).start()
    for t, (axis, n) in enumerate(tiles):
        if t + 1 < len(tiles):
            fetch(t + 1).start()
        fetch(t).wait()
        cut = slice(256 * n, 256 * (n + 1))
        for m in STEPS + (0,):
            both = jnp.dot(mixing[axis, m, :, 0:256], land[t % 2, m], preferred_element_type=F32)
            both = both + jnp.dot(mixing[axis, m, :, 256:512], land[t % 2, 4], preferred_element_type=F32)
            total = both[0:TOKENS] + both[TOKENS : 2 * TOKENS]
            if m == 0:
                at = PARTS[axis][1] + 256 * n
                own_sum[:, at : at + 256] = total
            else:
                lines[axis][TOKENS * m : TOKENS * (m + 1), cut] = total.astype(BF)
        if n in (2, PARTS[axis][2] // 256 - 1):
            half = slice(0, 768) if n == 2 else slice(768, PARTS[axis][2])
            for s, m in enumerate(STEPS):
                i = 3 * s + axis + (9 if n > 2 else 0)
                parts.append(
                    remote(
                        lines[axis].at[pl.ds(TOKENS * m, TOKENS), half], sums[axis].at[s, :, half],
                        sum_send.at[i], sum_recv.at[i], moved_back(line_offset(axis, m)),
                    )
                )
                parts[-1].start()
    for copy in last:
        copy.wait()
    for copy in parts:
        copy.wait()
    for axis, at, width in PARTS:
        total = own_sum[:, at : at + width]
        for s in range(3):
            total = total + sums[axis][s].astype(F32)
        work[0:TOKENS, at : at + width] = total.astype(BF)
    result = pltpu.make_async_copy(work.at[pl.ds(0, TOKENS)], mix_ref, local_sem.at[0])
    result.start()
    result.wait()


def body(
    queries, rotated_key_heads, stacked_value_heads, moe_rows, expert_ids, route_weights, w_gate, w_up, w_down
):
    hbm = pl.BlockSpec(memory_space=pl.ANY)
    dma = pltpu.SemaphoreType.DMA
    widths = [width for _, _, width in PARTS]
    results = pl.pallas_call(
        kernel,
        out_shape=(jax.ShapeDtypeStruct((SEQ, D), BF), jax.ShapeDtypeStruct((TOKENS, D), BF))
        + tuple(jax.ShapeDtypeStruct((5, 256, w), BF) for w in widths) * 2
        + tuple(jax.ShapeDtypeStruct((2, 3, 5, 32, w), BF) for w in widths) * 2,
        in_specs=[hbm] * 9,
        out_specs=(hbm,) * 14,
        scratch_shapes=[pltpu.VMEM((4 * TOKENS, w), BF) for w in widths]
        + [pltpu.VMEM((5, 256, w), BF) for w in widths]
        + [
            pltpu.VMEM((8, TOKENS), jnp.int32),
            pltpu.VMEM((8, TOKENS), F32),
            pltpu.VMEM((16, TOKENS), F32),
            pltpu.VMEM((3, 4, 16, TOKENS), F32),
            pltpu.VMEM((3, 256, 4 * TOKENS), BF),
            pltpu.VMEM((16, 4, 2, SEQ, 256), BF),
            pltpu.VMEM((4, SEQ, 1024), BF),
            pltpu.VMEM((16, 128, 512), BF),
            pltpu.VMEM((4, SEQ, 1024), BF),
            pltpu.VMEM((640, D), BF),
            pltpu.VMEM((D, FFE), BF),
            pltpu.VMEM((D, FFE), BF),
            pltpu.VMEM((FFE, D), BF),
            pltpu.VMEM((640, FFE), BF),
            pltpu.VMEM((2, 5, 256, 256), BF),
            pltpu.VMEM((3, 4, 2 * TOKENS, 512), BF),
        ]
        + [pltpu.VMEM((3, TOKENS, w), BF) for w in widths]
        + [pltpu.VMEM((TOKENS, D), F32)]
        + [dma((n,)) for n in (93, 93, 9, 9, 9, 9, 9, 9, 15, 15, 16, 16, 3, 3, 10)]
        + [dma((n,)) for n in (1, 3, 93, 93, 18, 18, 2, 18, 18, 12, 18, 18)],
        compiler_params=pltpu.CompilerParams(
            collective_id=0, has_side_effects=True, vmem_limit_bytes=62 * 2**20
        ),
        name="attend_and_mix",
    )(
        queries, rotated_key_heads, stacked_value_heads, moe_rows, expert_ids.T, route_weights.T,
        w_gate, w_up, w_down,
    )
    return results[0], results[1]


def solution(mesh):
    rows = P(("ctx", "exp"), None)
    cube = P(("ctx", "exp"), None, None)
    return jax.shard_map(
        body,
        mesh=mesh,
        in_specs=(rows,) * 6 + (cube,) * 3,
        out_specs=(rows, rows),
        check_vma=False,
    )
```

```python
import math

import jax
import jax.numpy as jnp
import numpy as np
from jax import lax
from jax.experimental import pallas as pl
from jax.experimental.pallas import tpu as pltpu
from jax.sharding import PartitionSpec as P

MESH = pl.DeviceIdType.MESH
BF = jnp.bfloat16
F32 = jnp.float32
D = 4096
FFE = 768
TOKENS = 128
SEQ = 64
PARTS = ((0, 0, 1536), (1, 1536, 1280), (2, 2816, 1280))
STEPS = (1, 3, 2)


def plane_offset(axis, i):
    d = [0, 0, 0]
    d[(axis + 1) % 3] = i // 4 % 4
    d[(axis + 2) % 3] = i % 4
    return tuple(d) + (i // 16,)


def line_offset(axis, m):
    d = [0, 0, 0, 0]
    d[axis] = m
    return tuple(d)


PEERS = sorted({plane_offset(p, i) for p in range(3) for i in range(1, 32)})


def place():
    c = lax.axis_index("ctx")
    e = lax.axis_index("exp")
    return c % 4, c // 4, e // 2, e % 2


def device(x, y, z, c):
    return (y * 4 + x, z * 2 + c)


def moved(d):
    x, y, z, c = place()
    return device((x + d[0]) % 4, (y + d[1]) % 4, (z + d[2]) % 4, (c + d[3]) % 2)


def moved_back(d):
    return moved(((-d[0]) % 4, (-d[1]) % 4, (-d[2]) % 4, d[3]))


def greet_all():
    barrier = pltpu.get_barrier_semaphore()
    for d in PEERS:
        pl.semaphore_signal(barrier, inc=1, device_id=moved(d), device_id_type=MESH)


def await_all():
    pl.semaphore_wait(pltpu.get_barrier_semaphore(), len(PEERS))


def remote(src, dst, send, recv, target):
    return pltpu.make_async_remote_copy(
        src_ref=src, dst_ref=dst, send_sem=send, recv_sem=recv, device_id=target, device_id_type=MESH
    )


def owners(axis):
    x, y, z, c = place()
    i = lax.broadcasted_iota(jnp.int32, (32, TOKENS), 0)
    d = [0, 0, 0]
    d[(axis + 1) % 3] = i // 4 % 4
    d[(axis + 2) % 3] = i % 4
    chip = ((y + d[1]) % 4 * 4 + (x + d[0]) % 4) * 4 + (z + d[2]) % 4
    return (chip * 2 + (c + i // 16) % 2).astype(F32)


def ranks(ids, owner):
    named = jnp.zeros((32, TOKENS), F32)
    for k in range(8):
        named = named + jnp.where(ids[k : k + 1, :] == owner, 1.0, 0.0)
    shape = (TOKENS, TOKENS)
    before = lax.broadcasted_iota(jnp.int32, shape, 0) < lax.broadcasted_iota(jnp.int32, shape, 1)
    rank = jnp.dot(named.astype(BF), jnp.where(before, 1.0, 0.0).astype(BF), preferred_element_type=F32)
    return jnp.where(named > 0.5, rank, -1.0)


def spread(a):
    return jnp.broadcast_to(a[:, None, :], (32, 8, TOKENS)).reshape(256, TOKENS)


def line_index():
    return lax.broadcasted_iota(jnp.int32, (256, TOKENS), 0) % 8


def slot_masks(rank, m):
    row, line = spread(rank), line_index()
    early = row == line.astype(F32)
    late = (row == (8 + line % 2).astype(F32)) & (line // 2 == m)
    return early, late


def reorder(axis, forward):
    a = lax.broadcasted_iota(jnp.int32, (128, 128), 0 if forward else 1)
    b = lax.broadcasted_iota(jnp.int32, (128, 128), 1 if forward else 0)
    dx, dy, dz, s = a // 32, a // 8 % 4, a // 2 % 4, a % 2
    there = (dy * 4 + dz) * 8 + dx * 2 + s if axis == 0 else (dz * 4 + dx) * 8 + dy * 2 + s
    return jnp.where(there == b, 1.0, 0.0).astype(BF)


def kernel(
    q_ref, k_ref, v_ref, rows_ref, ids_ref, weight_ref, gate_ref, up_ref, down_ref,
    att_ref, mix_ref, recv_a, recv_b, recv_c, came_a, came_b, came_c, mid_a, mid_b, mid_c,
    back_mid_a, back_mid_b, back_mid_c,
    line_a, line_b, line_c, pack_a, pack_b, pack_c, ids_here, weights_here, info, meta, late_hot,
    kv, queries, v_turned, heads_out, work, gate, up, down, hidden, land, mixing, sum_a, sum_b, sum_c, own_sum,
    send_sem, recv_sem, line_send, line_recv, meta_send, meta_recv, in_send, in_recv,
    kv_send, kv_recv, core_send, core_recv, out_send, out_recv, local_sem,
    load_sem, w_sem, back_send, back_recv, sum_send, sum_recv, land_sem,
    hop_send, hop_recv, stay_sem, back_hop_send, back_hop_recv,
):
    x, y, z, c = place()
    ctx = y * 4 + x
    lines, packs, recvs = (line_a, line_b, line_c), (pack_a, pack_b, pack_c), (recv_a, recv_b, recv_c)
    cames, sums, mids = (came_a, came_b, came_c), (sum_a, sum_b, sum_c), (mid_a, mid_b, mid_c)
    back_mids = (back_mid_a, back_mid_b, back_mid_c)
    greet_all()
    small = [
        pltpu.make_async_copy(ids_ref, ids_here, land_sem.at[0]),
        pltpu.make_async_copy(weight_ref, weights_here, land_sem.at[1]),
    ]
    for copy in small:
        copy.start()
    mine = [
        pltpu.make_async_copy(rows_ref.at[:, at : at + width], lines[axis].at[pl.ds(0, TOKENS)], local_sem.at[7 + axis])
        for axis, at, width in PARTS
    ]
    for copy in mine:
        copy.start()
    for copy in small:
        copy.wait()
    info[0:8, :] = ids_here[...].astype(F32)
    info[8:16, :] = weights_here[...]
    await_all()

    first = []
    for dz in range(4):
        zt = (z + dz) % 4
        for n, ref in enumerate((k_ref, v_ref)):
            there = ref.at[:, pl.ds(zt * 128, 128)]
            here = kv.at[ctx, z, c, :, pl.ds(128 * n, 128)]
            if dz == 0:
                first.append(pltpu.make_async_copy(there, here, local_sem.at[n]))
            else:
                i = (dz - 1) * 3 + n
                first.append(remote(there, here, in_send.at[i], in_recv.at[i], device(x, y, zt, c)))
            first[-1].start()

    along = {}
    for n, m in enumerate(STEPS):
        for axis, at, width in PARTS:
            target = moved(line_offset(axis, m))
            i = 3 * n + axis
            told = remote(info, meta.at[axis, m], meta_send.at[i], meta_recv.at[i], target)
            told.start()
            data = remote(
                rows_ref.at[:, at : at + width], lines[axis].at[pl.ds(TOKENS * m, TOKENS)],
                line_send.at[i], line_recv.at[i], target,
            )
            data.start()
            along[axis, m] = (told, data)

    asked = []
    for dz in range(4):
        zt = (z + dz) % 4
        there = q_ref.at[:, pl.ds(zt * 1024, 1024)]
        if dz == 0:
            asked.append(pltpu.make_async_copy(there, queries.at[z], local_sem.at[2]))
        else:
            i = (dz - 1) * 3 + 2
            asked.append(remote(there, queries.at[z], in_send.at[i], in_recv.at[i], device(x, y, zt, c)))
        asked[-1].start()

    for copy in first:
        copy.wait()
    for k in range(1, 16):

        @pl.when(ctx + k < 16)
        def _():
            there = ctx + k
            remote(
                kv.at[ctx, :, c], kv.at[ctx, :, c], kv_send.at[k - 1], kv_recv.at[k - 1], (there, z * 2 + c)
            ).start()

    weights = [
        pltpu.make_async_copy(gate_ref.at[0], gate, w_sem.at[0]),
        pltpu.make_async_copy(up_ref.at[0], up, w_sem.at[1]),
        pltpu.make_async_copy(down_ref.at[0], down, w_sem.at[2]),
    ]
    for copy in weights:
        copy.start()

    for m in (0,) + STEPS:
        for axis, at, width in PARTS:
            if m == 0:
                meta[axis, 0] = info[...]
                mine[axis].wait()
            else:
                for copy in along[axis, m]:
                    copy.wait()
            early, late = slot_masks(ranks(meta[axis, m], owners(axis)), m)
            hot = jnp.where(early, 1.0, 0.0).astype(BF)
            late_hot[axis, :, TOKENS * m : TOKENS * (m + 1)] = jnp.where(late, 1.0, 0.0).astype(BF)
            packs[axis][m] = jnp.dot(
                hot, lines[axis][TOKENS * m : TOKENS * (m + 1), :], preferred_element_type=F32
            ).astype(BF)
    for axis, at, width in PARTS:
        packs[axis][4] = jnp.dot(late_hot[axis], lines[axis][...], preferred_element_type=F32).astype(BF)

    hops = {}
    sends = ([], [])
    stays = []

    def hop(core):
        for d1 in STEPS:
            for axis in range(3):
                n = (axis * 2 + core) * 3 + d1 - 1
                hops[axis, core, d1] = remote(
                    packs[axis].at[:, pl.ds(8 * (16 * core + 4 * d1), 32)], mids[axis].at[core, d1 - 1],
                    hop_send.at[n], hop_recv.at[n], moved(line_offset((axis + 1) % 3, d1)),
                )
                hops[axis, core, d1].start()

    def leg(core, d1):
        for axis in range(3):
            if d1 > 0:
                hops[axis, core, d1].wait_recv()
            for d2 in STEPS + (0,):
                i = 16 * core + 4 * d1 + d2
                n = 31 * axis + i - 1
                here = pl.ds(8 * i, 8)
                from_ref = packs[axis].at[:, here] if d1 == 0 else mids[axis].at[core, d1 - 1, :, pl.ds(8 * d2, 8)]
                if core == 0 and d2 == 0:
                    copy = pltpu.make_async_copy(from_ref, recvs[axis].at[:, here], stay_sem.at[4 * axis + d1])
                    copy.start()
                    stays.append((axis, copy))
                else:
                    target = moved(line_offset((axis + 2) % 3, d2)[:3] + (core,))
                    copy = remote(from_ref, recvs[axis].at[:, here], send_sem.at[n], recv_sem.at[n], target)
                    copy.start()
                    sends[core].append((axis, copy))

    hop(0)
    leg(0, 0)
    hop(1)

    for copy in asked:
        copy.wait()
    for k in range(1, 16):
        copy = remote(
            kv.at[ctx, :, c], kv.at[ctx, :, c], kv_send.at[k - 1], kv_recv.at[k - 1], (ctx, z * 2 + c)
        )

        @pl.when(ctx >= k)
        def _():
            copy.wait_recv()

        @pl.when(ctx + k < 16)
        def _():
            copy.wait_send()

    def core_copy(j):
        return remote(
            kv.at[j, :, c], kv.at[j, :, c], core_send.at[j], core_recv.at[j], device(x, y, z, 1 - c)
        )

    def core_start(j, carry):
        core_copy(j).start()
        return carry

    def core_wait(j, carry):
        core_copy(j).wait()
        return carry

    lax.fori_loop(0, ctx + 1, core_start, 0)
    lax.fori_loop(0, ctx + 1, core_wait, 0)

    def turn(j, carry):
        block = kv[j].reshape(512, 256)
        v_turned[j] = block[:, 128:256].astype(F32).T.astype(BF)
        return carry

    lax.fori_loop(0, ctx + 1, turn, 0)
    factor = math.log2(math.e) / math.sqrt(128.0)
    column = lax.broadcasted_iota(jnp.int32, (512, 256), 1)
    allowed = lax.broadcasted_iota(jnp.int32, (512, 256), 0) <= (column // 64 * 2 + c) * 64 + column % 64

    def head(h, carry):
        cut = pl.ds(pl.multiple_of(h * 128, 128), 128)
        q = queries[:, :, cut].reshape(256, 128)

        def step(j, state, masked):
            row_max, row_sum, total = state
            key = kv[j].reshape(512, 256)[:, 0:128]
            score = lax.dot_general(key, q, (((1,), (1,)), ((), ())), preferred_element_type=F32) * factor
            if masked:
                score = jnp.where(allowed, score, -1e30)
            new_max = jnp.maximum(row_max, jnp.max(score, axis=0, keepdims=True))
            prob = jnp.exp2(score - new_max)
            old = jnp.exp2(row_max - new_max)
            row_sum = row_sum * old + jnp.sum(prob, axis=0, keepdims=True)
            total = total * old + jnp.dot(v_turned[j], prob.astype(BF), preferred_element_type=F32)
            return (new_max, row_sum, total)

        state = (
            jnp.full((1, 256), -1e30, F32),
            jnp.zeros((1, 256), F32),
            jnp.zeros((128, 256), F32),
        )
        state = step(ctx, state, True)
        state = lax.fori_loop(0, ctx, lambda j, s: step(j, s, False), state)
        result = (state[2] / state[1]).T
        heads_out[:, :, cut] = result.reshape(4, 64, 128).astype(BF)
        return carry

    for h, d1 in enumerate(STEPS):
        lax.fori_loop(h, h + 1, head, 0)
        leg(0, d1)
    leg(1, 0)
    lax.fori_loop(3, 5, head, 0)
    for d1 in STEPS:
        leg(1, d1)

    def load(core, axis):
        at = 128 * core
        _, left, width = PARTS[axis]
        columns = pl.ds(left, width)
        if axis == 0:
            for dx in range(4):
                pltpu.make_async_copy(
                    recv_a.at[dx, pl.ds(at, 128)], work.at[pl.ds(128 * dx, 128), columns], load_sem.at[0]
                ).start()
        else:

            def piece(n, carry):
                dx, dy, dz = n // 16, n // 4 % 4, n % 4
                m, block = (dy, dz * 4 + dx) if axis == 1 else (dz, dx * 4 + dy)
                pltpu.make_async_copy(
                    recvs[axis].at[m, pl.ds(pl.multiple_of(at + block * 8, 8), 8)],
                    work.at[pl.ds(pl.multiple_of(8 * n, 8), 8), columns],
                    load_sem.at[0],
                ).start()
                return carry

            lax.fori_loop(0, 64, piece, 0)
        pltpu.make_async_copy(
            recvs[axis].at[4, pl.ds(at, 128)], work.at[pl.ds(512, 128), columns], load_sem.at[0]
        ).start()

    legs = {}
    back_hops = []

    def back_leg(core, axis):
        for d1 in STEPS + (0,):
            for d2 in STEPS + (0,):
                i = 16 * core + 4 * d1 + d2
                n = 31 * axis + i - 1
                here = packs[axis].at[:, pl.ds(8 * i, 8)]
                there = (
                    cames[axis].at[:, pl.ds(8 * i, 8)]
                    if d1 == 0
                    else back_mids[axis].at[core, d1 - 1, :, pl.ds(8 * d2, 8)]
                )
                if core == 0 and d2 == 0:
                    copy = pltpu.make_async_copy(here, there, stay_sem.at[4 * axis + d1])
                else:
                    target = moved_back(line_offset((axis + 2) % 3, d2)[:3] + (core,))
                    copy = remote(here, there, back_send.at[n], back_recv.at[n], target)
                copy.start()
                legs[axis, core, d1, d2] = copy

    def back_hop(core, d1):
        for axis in range(3):
            for d2 in range(4):
                copy = legs[axis, core, d1, d2]
                if core == 0 and d2 == 0:
                    copy.wait()
                else:
                    copy.wait_recv()
            n = (axis * 2 + core) * 3 + d1 - 1
            back_hops.append(
                remote(
                    back_mids[axis].at[core, d1 - 1], cames[axis].at[:, pl.ds(8 * (16 * core + 4 * d1), 32)],
                    back_hop_send.at[n], back_hop_recv.at[n], moved_back(line_offset((axis + 1) % 3, d1)),
                )
            )
            back_hops[-1].start()

    for core in range(2):
        for axis in range(3):
            for part, copy in sends[core]:
                if part == axis:
                    copy.wait_recv()
            if core == 0:
                for part, copy in stays:
                    if part == axis:
                        copy.wait()
            load(core, axis)
        pltpu.make_async_copy(work, work, load_sem.at[0]).wait()
        if core == 0:
            weights[0].wait()
            weights[1].wait()
        for axis, at, width in PARTS[:2]:
            work[512:640, at : at + width] = jnp.dot(
                reorder(axis, True), work[512:640, at : at + width], preferred_element_type=F32
            ).astype(BF)

        def inner(n, carry):
            cut = pl.ds(pl.multiple_of(n * 256, 256), 256)
            a = jnp.dot(work[...], gate[:, cut], preferred_element_type=F32)
            b = jnp.dot(work[...], up[:, cut], preferred_element_type=F32)
            hidden[:, cut] = (a / (1.0 + jnp.exp(-a)) * b).astype(BF)
            return carry

        lax.fori_loop(0, 3, inner, 0)
        if core == 1:
            for d1 in STEPS:
                back_hop(0, d1)
        if core == 0:
            weights[2].wait()
        for copy in [hops[axis, core, d1] for axis in range(3) for d1 in STEPS] + [copy for _, copy in sends[core]]:
            copy.wait_send()
        for axis, at, width in PARTS:
            ref = packs[axis]

            def outer(n, carry):
                cut = pl.ds(pl.multiple_of(n * 256, 256), 256)
                from_cut = pl.ds(pl.multiple_of(at + n * 256, 256), 256)
                value = jnp.dot(hidden[...], down[:, from_cut], preferred_element_type=F32)
                row = 128 * core
                if axis == 0:
                    for dx in range(4):
                        ref[dx, row : row + 128, cut] = value[128 * dx : 128 * (dx + 1)].astype(BF)
                elif axis == 1:
                    for n2 in range(64):
                        to = row + (n2 % 4 * 4 + n2 // 16) * 8
                        ref[n2 // 4 % 4, to : to + 8, cut] = value[8 * n2 : 8 * (n2 + 1)].astype(BF)
                else:
                    for n2 in range(64):
                        to = row + n2 // 4 * 8
                        ref[n2 % 4, to : to + 8, cut] = value[8 * n2 : 8 * (n2 + 1)].astype(BF)
                late = value[512:640].astype(BF)
                if axis < 2:
                    late = jnp.dot(reorder(axis, False), late, preferred_element_type=F32).astype(BF)
                ref[4, row : row + 128, cut] = late
                return carry

            lax.fori_loop(0, width // 256, outer, 0)
            back_leg(core, axis)
    for axis, at, width in PARTS:
        for m in range(4):
            early, late = slot_masks(ranks(meta[axis, m], owners(axis)), m)
            value = jnp.zeros((32, TOKENS), F32)
            for k in range(8):
                value = value + jnp.where(
                    meta[axis, m, k : k + 1, :] == owners(axis), meta[axis, m, 8 + k : 9 + k, :], 0.0
                )
            value = spread(value)
            for n, mask in enumerate((early, late)):
                turned = jnp.where(mask, value, 0.0).T
                high = turned.astype(BF)
                mixing[axis, m, 0:TOKENS, 256 * n : 256 * (n + 1)] = high
                mixing[axis, m, TOKENS : 2 * TOKENS, 256 * n : 256 * (n + 1)] = (turned - high.astype(F32)).astype(BF)
    lax.fori_loop(5, 7, head, 0)
    for d1 in STEPS:
        back_hop(1, d1)
    lax.fori_loop(7, 8, head, 0)
    last = []
    for dz in range(1, 4):
        zt = (z + dz) % 4
        last.append(
            remote(
                heads_out.at[zt], att_ref.at[:, pl.ds(z * 1024, 1024)],
                out_send.at[dz - 1], out_recv.at[dz - 1], device(x, y, zt, c),
            )
        )
        last[-1].start()
    last.append(pltpu.make_async_copy(heads_out.at[z], att_ref.at[:, pl.ds(z * 1024, 1024)], local_sem.at[6]))
    last[-1].start()
    for (axis, core, d1, d2), copy in legs.items():
        if core == 0 and d2 == 0:
            if d1 == 0:
                copy.wait()
        else:
            copy.wait_send()
            if d1 == 0:
                copy.wait_recv()
    for copy in back_hops:
        copy.wait()

    groups = [(axis, n) for n in (0, 3) for axis in range(3)]
    tiles = [
        (axis, n) for axis, first_tile in groups for n in range(first_tile, min(first_tile + 3, PARTS[axis][2] // 256))
    ]

    def fetch(t):
        axis, n = tiles[t]
        return pltpu.make_async_copy(
            cames[axis].at[:, :, 256 * n : 256 * (n + 1)], land.at[t % 2], land_sem.at[t % 2]
        )

    parts = []
    fetch(0).start()
    for t, (axis, n) in enumerate(tiles):
        if t + 1 < len(tiles):
            fetch(t + 1).start()
        fetch(t).wait()
        cut = slice(256 * n, 256 * (n + 1))
        for m in STEPS + (0,):
            both = jnp.dot(mixing[axis, m, :, 0:256], land[t % 2, m], preferred_element_type=F32)
            both = both + jnp.dot(mixing[axis, m, :, 256:512], land[t % 2, 4], preferred_element_type=F32)
            total = both[0:TOKENS] + both[TOKENS : 2 * TOKENS]
            if m == 0:
                at = PARTS[axis][1] + 256 * n
                own_sum[:, at : at + 256] = total
            else:
                lines[axis][TOKENS * m : TOKENS * (m + 1), cut] = total.astype(BF)
        if n in (2, PARTS[axis][2] // 256 - 1):
            half = slice(0, 768) if n == 2 else slice(768, PARTS[axis][2])
            for s, m in enumerate(STEPS):
                i = 3 * s + axis + (9 if n > 2 else 0)
                parts.append(
                    remote(
                        lines[axis].at[pl.ds(TOKENS * m, TOKENS), half], sums[axis].at[s, :, half],
                        sum_send.at[i], sum_recv.at[i], moved_back(line_offset(axis, m)),
                    )
                )
                parts[-1].start()
    for copy in last:
        copy.wait()
    for copy in parts:
        copy.wait()
    for axis, at, width in PARTS:
        total = own_sum[:, at : at + width]
        for s in range(3):
            total = total + sums[axis][s].astype(F32)
        work[0:TOKENS, at : at + width] = total.astype(BF)
    result = pltpu.make_async_copy(work.at[pl.ds(0, TOKENS)], mix_ref, local_sem.at[0])
    result.start()
    result.wait()


def body(
    queries, rotated_key_heads, stacked_value_heads, moe_rows, expert_ids, route_weights, w_gate, w_up, w_down
):
    hbm = pl.BlockSpec(memory_space=pl.ANY)
    dma = pltpu.SemaphoreType.DMA
    widths = [width for _, _, width in PARTS]
    results = pl.pallas_call(
        kernel,
        out_shape=(jax.ShapeDtypeStruct((SEQ, D), BF), jax.ShapeDtypeStruct((TOKENS, D), BF))
        + tuple(jax.ShapeDtypeStruct((5, 256, w), BF) for w in widths) * 2
        + tuple(jax.ShapeDtypeStruct((2, 3, 5, 32, w), BF) for w in widths) * 2,
        in_specs=[hbm] * 9,
        out_specs=(hbm,) * 14,
        scratch_shapes=[pltpu.VMEM((4 * TOKENS, w), BF) for w in widths]
        + [pltpu.VMEM((5, 256, w), BF) for w in widths]
        + [
            pltpu.VMEM((8, TOKENS), jnp.int32),
            pltpu.VMEM((8, TOKENS), F32),
            pltpu.VMEM((16, TOKENS), F32),
            pltpu.VMEM((3, 4, 16, TOKENS), F32),
            pltpu.VMEM((3, 256, 4 * TOKENS), BF),
            pltpu.VMEM((16, 4, 2, SEQ, 256), BF),
            pltpu.VMEM((4, SEQ, 1024), BF),
            pltpu.VMEM((16, 128, 512), BF),
            pltpu.VMEM((4, SEQ, 1024), BF),
            pltpu.VMEM((640, D), BF),
            pltpu.VMEM((D, FFE), BF),
            pltpu.VMEM((D, FFE), BF),
            pltpu.VMEM((FFE, D), BF),
            pltpu.VMEM((640, FFE), BF),
            pltpu.VMEM((2, 5, 256, 256), BF),
            pltpu.VMEM((3, 4, 2 * TOKENS, 512), BF),
        ]
        + [pltpu.VMEM((3, TOKENS, w), BF) for w in widths]
        + [pltpu.VMEM((TOKENS, D), F32)]
        + [dma((n,)) for n in (93, 93, 9, 9, 9, 9, 9, 9, 15, 15, 16, 16, 3, 3, 10)]
        + [dma((n,)) for n in (1, 3, 93, 93, 18, 18, 2, 18, 18, 12, 18, 18)],
        compiler_params=pltpu.CompilerParams(
            collective_id=0, has_side_effects=True, vmem_limit_bytes=62 * 2**20
        ),
        name="attend_and_mix",
    )(
        queries, rotated_key_heads, stacked_value_heads, moe_rows, expert_ids.T, route_weights.T,
        w_gate, w_up, w_down,
    )
    return results[0], results[1]


def solution(mesh):
    rows = P(("ctx", "exp"), None)
    cube = P(("ctx", "exp"), None, None)
    return jax.shard_map(
        body,
        mesh=mesh,
        in_specs=(rows,) * 6 + (cube,) * 3,
        out_specs=(rows, rows),
        check_vma=False,
    )
```
